128 devices in a mesh: gx: 32 (over z, y, core), gz: 4 (over x).
Axes of the slice: x: 4, y: 4, z: 4, core: 2. Of those that a mesh axis runs over, the one named last changes fastest.
Arguments:
- parents: bfloat16 [35, 8, 524288], P(None, None, ('gx', 'gz')), may hold values from -6 to 6
- refine: int32 [524288], P(('gx', 'gz')), may hold values 0 or 1
- edge: int32 [524288], P(('gx', 'gz')), may hold values from 0 to 5
- move: int32 [524288], P(('gx', 'gz')), may hold values from 0 to 6, as said below
- face_owner: int32 [4, 128, 1024], P(None, ('gx', 'gz')), may hold values from 0 to 4095
- face_local: int32 [4, 128, 1024], P(None, ('gx', 'gz')), may hold values from 0 to 3
- face_pair: int32 [4, 128, 1024], P(None, ('gx', 'gz')), may hold values from 0 to 1023, each once within a row
- face_orient: int32 [4, 128, 1024], P(None, ('gx', 'gz')), may hold values from 0 to 5
- prolong: bfloat16 [6, 2, 35, 35], replicated, may hold values from -1 to 1
- restrict: bfloat16 [4, 15, 35], replicated, may hold values from -1 to 1
- lift: float32 [4, 35, 15], replicated, may hold values from -1.5 to 1.5
Outputs:
- migrated: bfloat16 [2, 35, 8, 720896], P(None, None, None, ('gx', 'gz'))
The draws below stay inside these ranges and needn't reach their ends.
Inputs may be any that keep to these rules, and one draw needn't show every extreme that they name: Each row of face_pair is a permutation of the neighbour's 1024 faces on the matching side. Among the 4096 parents of one device at most 256 have the same move k < 6, and on every device some k reaches exactly 256.
All inputs are finite; a program needn't handle non-finite values. No bound on the sum of `refine` on one device may be relied on, other than what follows from the above.
Results may differ from the reference program's by a relative error of at most 0.005.
Values may be sent and summed in bfloat16 or wider, within the bound.
No kernel may reach another device: no remote copies, remote signals or barrier semaphores. Data moves between devices by JAX's collectives and lax.ppermute only.
A program may use at most 128 MiB of HBM per device.

```python
import jax
import jax.numpy as jnp
import numpy as np
from jax import lax

MODES = 35
FMODES = 15
FIELDS = 8
P_DEV = 4096
F_DEV = 1024
CAP = 256
SLOTS = 5632
PARENTS = 524288
N_GX = 32
N_GZ = 4
DEVICES = 128


def draw_move(key, part):

    def one_device(index):
        device_key = jax.random.fold_in(jax.random.fold_in(key, 7001), index)
        count_key, full_key, order_key = jax.random.split(device_key, 3)
        counts = jax.random.randint(count_key, (6,), CAP // 2, CAP + 1)
        full = jax.random.randint(full_key, (), 0, 6)
        counts = jnp.where(jnp.arange(6, dtype=jnp.int32) == full, CAP, counts).astype(jnp.int32)
        bounds = jnp.cumsum(counts)
        code_at = jnp.sum((jnp.arange(P_DEV, dtype=jnp.int32)[:, None] >= bounds[None, :]).astype(jnp.int32), axis=1)
        order = jax.random.permutation(order_key, P_DEV)
        return jnp.zeros((P_DEV,), jnp.int32).at[order].set(code_at.astype(jnp.int32))
    return jax.vmap(one_device)(jnp.arange(DEVICES, dtype=jnp.int32)).reshape(-1)


def touch_ends(drawn, own_key, least, top_value):
    spot = [jax.random.randint(jax.random.fold_in(own_key, axis), (), 0, length) for axis, length in enumerate(drawn.shape)]
    main_axis = drawn.shape.index(max(drawn.shape))
    next_to = spot[:main_axis] + [(spot[main_axis] + 1) % drawn.shape[main_axis]] + spot[main_axis + 1:]
    return drawn.at[tuple(spot)].set(least).at[tuple(next_to)].set(top_value)


def level_of(stream_key, extent, pieces, smallest, top_value):
    level = 1.0
    for axis_at, blocks in pieces:
        draws = jax.random.uniform(jax.random.fold_in(jax.random.fold_in(stream_key, 6), axis_at), (blocks,), jnp.float32, smallest / len(pieces), top_value / len(pieces))
        level = level * jnp.repeat(jnp.exp(draws), extent[axis_at] // blocks).reshape((-1,) + (1,) * (len(extent) - 1 - axis_at))
    return level


def normal_values(key, shape, spread, most, shards=(), kind=jnp.bfloat16):
    factor_of = level_of(key, shape, shards, -0.22, 0.18) if shards else 1.0
    entries = jax.random.normal(key, shape, jnp.float32) * spread * factor_of
    return jnp.minimum(jnp.maximum(entries, -most), most).astype(kind)


def setup_inputs(seed: int = 0) -> dict:
    arg_keys = jax.random.split(jax.random.key(seed), 12)
    parents = normal_values(arg_keys[0], (MODES, FIELDS, PARENTS), 1.0, 6.0, ((2, 128),))
    refine = touch_ends((jax.random.randint(arg_keys[1], (PARENTS,), 0, 4) < 3).astype(jnp.int32), jax.random.fold_in(arg_keys[1], 1), 0, 1)
    edge = touch_ends(jax.random.randint(arg_keys[2], (PARENTS,), 0, 6), jax.random.fold_in(arg_keys[2], 1), 0, 5).astype(jnp.int32)
    move = draw_move(jax.random.fold_in(arg_keys[11], 71), 0)
    face_owner = touch_ends(jax.random.randint(arg_keys[4], (4, DEVICES, F_DEV), 0, P_DEV), jax.random.fold_in(arg_keys[4], 1), 0, P_DEV - 1).astype(jnp.int32)
    face_local = touch_ends(jax.random.randint(arg_keys[5], (4, DEVICES, F_DEV), 0, 4), jax.random.fold_in(arg_keys[5], 1), 0, 3).astype(jnp.int32)
    face_pair = jax.vmap(lambda own: jax.random.permutation(own, F_DEV))(jax.random.split(arg_keys[6], 4 * DEVICES)).reshape((4, DEVICES, F_DEV)).astype(jnp.int32)
    face_orient = touch_ends(jax.random.randint(arg_keys[7], (4, DEVICES, F_DEV), 0, 6), jax.random.fold_in(arg_keys[7], 1), 0, 5).astype(jnp.int32)
    prolong = normal_values(arg_keys[8], (6, 2, MODES, MODES), MODES ** -0.5, 1.0)
    restrict = normal_values(arg_keys[9], (4, FMODES, MODES), MODES ** -0.5, 1.0)
    lift = normal_values(arg_keys[10], (4, MODES, FMODES), FMODES ** -0.5, 1.5, (), jnp.float32)
    return dict(parents=parents, refine=refine, edge=edge, move=move, face_owner=face_owner, face_local=face_local, face_pair=face_pair, face_orient=face_orient, prolong=prolong, restrict=restrict, lift=lift)


HIGH = lax.Precision.HIGHEST


def face_table():
    nodes = [(a, b, 4 - a - b) for a in range(5) for b in range(5 - a)]
    index = {node: place for place, node in enumerate(nodes)}
    orders = [(0, 1, 2), (1, 2, 0), (2, 0, 1), (1, 0, 2), (0, 2, 1), (2, 1, 0)]
    return np.array([[index[(n[p[0]], n[p[1]], n[p[2]])] for n in nodes] for p in orders], dtype=np.int32)


def side_select(local):
    return (local[None, :, :] == jnp.arange(4, dtype=jnp.int32)[:, None, None]).astype(jnp.float32)


def trace_block(block, owner, local, restrict):
    faces = owner.shape[1]
    picked = jnp.take(block, owner.reshape(-1), axis=2).reshape(MODES, FIELDS, 4, faces)
    every = jnp.einsum('lnm,mfsk->lnfsk', restrict.astype(jnp.float32), picked.astype(jnp.float32), precision=HIGH)
    chosen = jnp.sum(every * side_select(local)[:, None, None, :, :], axis=0)
    return chosen.transpose(2, 0, 1, 3).astype(jnp.bfloat16)


def correct_block(block, own, near, owner, local, pair, orient, lift):
    faces = owner.shape[1]
    paired = jnp.take_along_axis(near, pair[:, None, None, :], axis=3)
    variants = paired[:, jnp.asarray(face_table())]
    pick = (orient[:, None, :] == jnp.arange(6, dtype=jnp.int32)[None, :, None]).astype(jnp.float32)
    oriented = jnp.sum(variants.astype(jnp.float32) * pick[:, :, None, None, :], axis=1)
    jump = 0.5 * (oriented - own.astype(jnp.float32))
    lifted = jnp.einsum('lmn,snfk->lsmfk', lift, jump, precision=HIGH)
    summed = jnp.sum(lifted * side_select(local)[:, :, None, None, :], axis=0)
    summed = summed.transpose(1, 2, 0, 3).reshape(MODES, FIELDS, 4 * faces)
    total = jnp.zeros((MODES, FIELDS, block.shape[2]), jnp.float32).at[:, :, owner.reshape(-1)].add(summed)
    return (block.astype(jnp.float32) + total).astype(jnp.bfloat16)


def prolong_block(block, cut, flag, prolong):
    count = block.shape[2]
    flat = block.reshape(MODES, FIELDS * count)
    columns = jnp.broadcast_to(cut[None, :], (FIELDS, count)).reshape(-1)
    stacked = prolong.reshape(6, 2 * MODES, MODES)
    result = jnp.zeros((2 * MODES, FIELDS * count), jnp.float32)
    for which in range(6):
        product = jnp.dot(stacked[which], flat, preferred_element_type=jnp.float32)
        result = jnp.where(columns[None, :] == which, product, result)
    split = result.reshape(2, MODES, FIELDS, count)
    keep = jnp.stack([block.astype(jnp.float32), jnp.zeros(block.shape, jnp.float32)])
    return jnp.where(flag[None, None, None, :] == 1, split, keep).astype(jnp.bfloat16)


def rank_block(code):
    onehot = (code[:, None] == jnp.arange(6, dtype=jnp.int32)[None, :]).astype(jnp.int32)
    running = jnp.cumsum(onehot, axis=0)
    return (jnp.sum(onehot * running, axis=1) - 1).astype(jnp.int32)


def reference(parents, refine, edge, move, face_owner, face_local, face_pair, face_orient, prolong, restrict, lift):
    devices = N_GX * N_GZ
    blocks = parents.reshape(MODES, FIELDS, devices, P_DEV).transpose(2, 0, 1, 3)
    owner = face_owner.transpose(1, 0, 2)
    local = face_local.transpose(1, 0, 2)
    pair = face_pair.transpose(1, 0, 2)
    orient = face_orient.transpose(1, 0, 2)
    own = lax.map(lambda a: trace_block(a[0], a[1], a[2], restrict), (blocks, owner, local))
    grid = own.reshape(N_GX, N_GZ, 4, FMODES, FIELDS, F_DEV)
    near = jnp.stack([jnp.roll(grid[:, :, 1], 1, axis=0), jnp.roll(grid[:, :, 0], -1, axis=0),
                      jnp.roll(grid[:, :, 3], 1, axis=1), jnp.roll(grid[:, :, 2], -1, axis=1)], axis=2)
    near = near.reshape(devices, 4, FMODES, FIELDS, F_DEV)
    corrected = lax.map(lambda a: correct_block(a[0], a[1], a[2], a[3], a[4], a[5], a[6], lift),
                        (blocks, own, near, owner, local, pair, orient))
    kids = lax.map(lambda a: prolong_block(a[0], a[1], a[2], prolong),
                   (corrected, edge.reshape(devices, P_DEV), refine.reshape(devices, P_DEV)))
    code = move.reshape(devices, P_DEV)
    rank = lax.map(rank_block, code)
    source = jnp.broadcast_to(jnp.arange(devices, dtype=jnp.int32)[:, None], (devices, P_DEV))
    position = jnp.broadcast_to(jnp.arange(P_DEV, dtype=jnp.int32)[None, :], (devices, P_DEV))
    table = jnp.array([1, 2, 3, -1, -2, -3], dtype=jnp.int32)
    moving = code < 6
    offset = jnp.where(moving, jnp.take(table, jnp.minimum(code, 5)), 0).astype(jnp.int32)
    target = ((source + offset + devices) % devices).astype(jnp.int32)
    slot = jnp.where(moving, P_DEV + code * CAP + rank, position).astype(jnp.int32)
    values = kids.transpose(1, 2, 3, 0, 4).reshape(2, MODES, FIELDS, devices * P_DEV)
    result = jnp.zeros((2, MODES, FIELDS, devices, SLOTS), jnp.bfloat16)
    result = result.at[:, :, :, target.reshape(-1), slot.reshape(-1)].set(values)
    return result.reshape(2, MODES, FIELDS, devices * SLOTS)
```

```python
import jax
import jax.numpy as jnp
import numpy as np
from jax import lax
from jax.sharding import PartitionSpec as P

MODES = 35
FIELDS = 8


HIGH = lax.Precision.HIGHEST
OFFSETS = (1, 2, 3, -1, -2, -3)


def for_sending(array):

    def short(part):
        return part.astype(jnp.bfloat16) if part.dtype == jnp.float32 else part

    return jax.tree.map(short, array)


def passed_along(block, axis, distance):
    devices = range(lax.axis_size(axis))
    route = [((i - distance) % len(devices), i) for i in devices]
    return lax.ppermute(block, axis, route)


def padded(cells, sides, width):
    for axis, dim in sides:
        count = lax.axis_size(axis)
        head = lax.slice_in_dim(cells, 0, width, axis=dim)
        tail = lax.slice_in_dim(cells, cells.shape[dim] - width, cells.shape[dim], axis=dim)
        cells = jnp.concatenate(
            [
                lax.ppermute(tail, axis, [(i, (i + 1) % count) for i in range(count)]),
                cells,
                lax.ppermute(head, axis, [((i + 1) % count, i) for i in range(count)]),
            ],
            axis=dim,
        )
    return cells


def face_table():
    nodes = [(a, b, 4 - a - b) for a in range(5) for b in range(5 - a)]
    index = {node: place for place, node in enumerate(nodes)}
    orders = [(0, 1, 2), (1, 2, 0), (2, 0, 1), (1, 0, 2), (0, 2, 1), (2, 1, 0)]
    return np.array(
        [[index[n[p[0]], n[p[1]], n[p[2]]] for n in nodes] for p in orders], dtype=np.int32
    )


def side_select(local):
    return (local[None, :, :] == jnp.arange(4, dtype=jnp.int32)[:, None, None]).astype(jnp.float32)


def trace_block(block, owner, local, restrict, selector):
    faces = owner.shape[1]
    count = block.shape[2]
    flat = block.reshape(MODES * FIELDS, count)
    picked = jnp.dot(flat, selector, preferred_element_type=jnp.float32).astype(jnp.bfloat16)
    picked = picked.reshape(MODES, FIELDS, 4, faces)
    every = jnp.einsum("lnm,mfsk->lnfsk", restrict, picked, preferred_element_type=jnp.float32)
    chosen = jnp.sum(every * side_select(local)[:, None, None, :, :], axis=0)
    return chosen.transpose(2, 0, 1, 3).astype(jnp.bfloat16)


def correct_block(block, own, near, owner, local, pair, orient, lift, selector):
    faces = owner.shape[1]
    count = block.shape[2]
    matcher = (pair[:, None, :] == jnp.arange(faces, dtype=jnp.int32)[None, :, None]).astype(
        jnp.bfloat16
    )
    paired = jnp.einsum("snfj,sjk->snfk", near, matcher, preferred_element_type=jnp.float32)
    variants = paired[:, jnp.asarray(face_table())]
    pick = (orient[:, None, :] == jnp.arange(6, dtype=jnp.int32)[None, :, None]).astype(jnp.float32)
    oriented = jnp.sum(variants * pick[:, :, None, None, :], axis=1)
    jump = 0.5 * (oriented - own.astype(jnp.float32))
    lifted = jnp.einsum(
        "lmn,snfk->lsmfk",
        lift.astype(jnp.bfloat16),
        jump.astype(jnp.bfloat16),
        preferred_element_type=jnp.float32,
    )
    summed = jnp.sum(lifted * side_select(local)[:, :, None, None, :], axis=0)
    summed = summed.transpose(1, 2, 0, 3).reshape(MODES * FIELDS, 4 * faces)
    total = jnp.dot(
        summed.astype(jnp.bfloat16), selector.T, preferred_element_type=jnp.float32
    ).reshape(MODES, FIELDS, count)
    return (block.astype(jnp.float32) + total).astype(jnp.bfloat16)


def prolong_block(block, cut, flag, prolong):
    count = block.shape[2]
    flat = block.reshape(MODES, FIELDS * count)
    columns = jnp.broadcast_to(cut[None, :], (FIELDS, count)).reshape(-1)
    stacked = prolong.reshape(6, 2 * MODES, MODES)
    result = jnp.zeros((2 * MODES, FIELDS * count), jnp.float32)
    for which in range(6):
        product = jnp.dot(stacked[which], flat, preferred_element_type=jnp.float32)
        result = jnp.where(columns[None, :] == which, product, result)
    split = result.reshape(2, MODES, FIELDS, count)
    keep = jnp.stack([block.astype(jnp.float32), jnp.zeros(block.shape, jnp.float32)])
    return jnp.where(flag[None, None, None, :] == 1, split, keep).astype(jnp.bfloat16)


def shards(
    parents,
    refine,
    edge,
    move,
    face_owner,
    face_local,
    face_pair,
    face_orient,
    prolong,
    restrict,
    lift,
):
    count = parents.shape[2]
    capacity = count // 16
    owner = face_owner[:, 0, :]
    local = face_local[:, 0, :]
    selector = (jnp.arange(count, dtype=jnp.int32)[:, None] == owner.reshape(-1)[None, :]).astype(
        jnp.bfloat16
    )
    own = trace_block(parents, owner, local, restrict, selector)
    stream = padded(own[0:2], (("gx", 0),), 1)
    span = padded(own[2:4], (("gz", 0),), 1)
    near = jnp.stack([stream[0], stream[3], span[0], span[3]])
    corrected = correct_block(
        parents, own, near, owner, local, face_pair[:, 0, :], face_orient[:, 0, :], lift, selector
    )
    onehot = (move[:, None] == jnp.arange(6, dtype=jnp.int32)[None, :]).astype(jnp.int32)
    rank = jnp.sum(onehot * jnp.cumsum(onehot, axis=0), axis=1) - 1
    staying = move == 6
    place = jnp.where(staying, 6 * capacity, move * capacity + rank)
    packer = (place[:, None] == jnp.arange(6 * capacity, dtype=jnp.int32)[None, :]).astype(
        jnp.bfloat16
    )
    code = jnp.where(refine == 1, edge + 1, 0).astype(jnp.bfloat16)
    flat = corrected.reshape(MODES * FIELDS, count)
    payload = jnp.concatenate([flat, jnp.broadcast_to(code[None, :], (8, count))], axis=0)
    packed = jnp.dot(payload, packer, preferred_element_type=jnp.float32).astype(jnp.bfloat16)
    home = jnp.where(staying[None, None, :], corrected, jnp.zeros_like(corrected))
    home_kids = prolong_block(home, edge, refine, prolong)
    arrived = jnp.concatenate(
        [
            passed_along(packed[:, w * capacity : (w + 1) * capacity], ("gx", "gz"), OFFSETS[w])
            for w in range(6)
        ],
        axis=1,
    )
    incoming = arrived[: MODES * FIELDS].reshape(MODES, FIELDS, 6 * capacity)
    got = arrived[MODES * FIELDS].astype(jnp.int32)
    new_kids = prolong_block(incoming, got - 1, jnp.minimum(got, 1), prolong)
    return jnp.concatenate([home_kids, new_kids], axis=3)


def solution(mesh):
    in_specs = (
        P(None, None, ("gx", "gz")),
        P(("gx", "gz")),
        P(("gx", "gz")),
        P(("gx", "gz")),
        P(None, ("gx", "gz"), None),
        P(None, ("gx", "gz"), None),
        P(None, ("gx", "gz"), None),
        P(None, ("gx", "gz"), None),
        P(),
        P(),
        P(),
    )
    out_specs = P(None, None, None, ("gx", "gz"))
    return jax.shard_map(shards, mesh=mesh, in_specs=in_specs, out_specs=out_specs, check_vma=False)
```

```python
import functools

import jax
import jax.numpy as jnp
import numpy as np
from jax import lax
from jax.experimental import pallas as pl
from jax.experimental.pallas import tpu as pltpu
from jax.sharding import PartitionSpec as P

MODES = 35
FMODES = 15
FIELDS = 8
ROWS = MODES * FIELDS
NODE_ROWS = FMODES * FIELDS
PAD = 40
LANES = 128
OFFSETS = (1, 2, 3, -1, -2, -3)
F32 = jnp.float32
BF16 = jnp.bfloat16
NT = (((1,), (1,)), ((), ()))


def passed_along(block, axis, distance):
    count = lax.axis_size(axis)
    return lax.ppermute(block, axis, [((i - distance) % count, i) for i in range(count)])


def face_table():
    nodes = [(a, b, 4 - a - b) for a in range(5) for b in range(5 - a)]
    index = {node: place for place, node in enumerate(nodes)}
    orders = [(0, 1, 2), (1, 2, 0), (2, 0, 1), (1, 0, 2), (0, 2, 1), (2, 1, 0)]
    return [[index[n[p[0]], n[p[1]], n[p[2]]] for n in nodes] for p in orders]


def iota(shape, dim):
    return lax.broadcasted_iota(jnp.int32, shape, dim)


def ones_where(mask):
    return jnp.where(mask, 1.0, 0.0).astype(BF16)


def dot(a, b):
    return jnp.dot(a, b, preferred_element_type=F32)


def spread(small, rows, columns):
    height, width = small.shape
    left = ones_where(iota((rows, height), 0) // FIELDS == iota((rows, height), 1))
    right = ones_where(iota((width, columns), 0) == iota((width, columns), 1) // FIELDS)
    full = dot(dot(left, small).astype(BF16), right)
    same = iota((rows, columns), 0) % FIELDS == iota((rows, columns), 1) % FIELDS
    return jnp.where(same, full, 0.0)


def trace_kernel(tile, x_ref, owner_ref, local_ref, restrict_ref, own_ref):
    count = x_ref.shape[1]
    faces = owner_ref.shape[2]
    spreads = [spread(restrict_ref[l], NODE_ROWS, ROWS) for l in range(4)]
    every = jnp.concatenate(spreads, axis=0).astype(BF16)
    per = faces // tile

    def step(j, carry):
        s = j // per
        lanes = pl.ds(pl.multiple_of((j % per) * tile, tile), tile)
        owner = owner_ref[s, :, lanes]
        local = local_ref[s, :, lanes]
        onehot = ones_where(iota((count, tile), 0) == owner)
        picked = dot(x_ref[...], onehot).astype(BF16)
        traces = dot(every, picked)
        chosen = jnp.zeros((NODE_ROWS, tile), F32)
        for l in range(4):
            chosen = jnp.where(local == l, traces[l * NODE_ROWS : (l + 1) * NODE_ROWS], chosen)
        own_ref[s, :, lanes] = chosen.astype(BF16)
        return carry

    lax.fori_loop(0, 4 * per, step, 0)


def trace_call(x, owner, local, restrict):
    faces = owner.shape[2]
    return pl.pallas_call(
        functools.partial(trace_kernel, 512),
        out_shape=jax.ShapeDtypeStruct((4, NODE_ROWS, faces), BF16),
        compiler_params=pltpu.CompilerParams(vmem_limit_bytes=48 << 20),
        name="trace",
    )(x, owner, local, restrict)


def correct_kernel(
    tile,
    x_ref,
    own_ref,
    near0,
    near1,
    near2,
    near3,
    owner_ref,
    local_ref,
    pair_ref,
    orient_ref,
    lift_ref,
    place_ref,
    code_ref,
    fixed_ref,
    pack0,
    pack1,
    pack2,
    pack3,
    pack4,
    pack5,
    lifted_ref,
    payload_ref,
):
    count = x_ref.shape[1]
    faces = owner_ref.shape[2]
    cap = pack0.shape[1]
    table = face_table()
    raised = [spread(lift_ref[l].astype(BF16), ROWS, NODE_ROWS).astype(BF16) for l in range(4)]
    for s, near_ref in enumerate((near0, near1, near2, near3)):

        def jumps(j, carry, s=s, near_ref=near_ref):
            lanes = pl.ds(pl.multiple_of(j * tile, tile), tile)
            pair = pair_ref[s, :, lanes]
            orient = orient_ref[s, :, lanes]
            local = local_ref[s, :, lanes]
            matcher = ones_where(iota((faces, tile), 0) == pair)
            paired = dot(near_ref[...], matcher)
            own = own_ref[s, :, lanes].astype(F32)
            total = jnp.zeros((ROWS, tile), F32)
            jump = []
            for n in range(FMODES):
                best = paired[table[0][n] * FIELDS : (table[0][n] + 1) * FIELDS]
                for o in range(1, 6):
                    if table[o][n] != table[0][n]:
                        other = paired[table[o][n] * FIELDS : (table[o][n] + 1) * FIELDS]
                        best = jnp.where(orient == o, other, best)
                jump.append(0.5 * (best - own[n * FIELDS : (n + 1) * FIELDS]))
            jump = jnp.concatenate(jump, axis=0)
            for l in range(4):
                total += dot(raised[l], jnp.where(local == l, jump, 0.0).astype(BF16))
            at = pl.ds(pl.multiple_of(s * faces + j * tile, tile), tile)
            lifted_ref[:, at] = total.astype(BF16)
            return carry

        lax.fori_loop(0, faces // tile, jumps, 0)

    def fix(t, carry):
        at = pl.ds(pl.multiple_of(t * tile, tile), tile)
        total = x_ref[:, at].astype(F32)
        for s in range(4):
            selector = ones_where(iota((tile, faces), 0) + t * tile == owner_ref[s])
            total += lax.dot_general(
                lifted_ref[:, s * faces : (s + 1) * faces], selector, NT, preferred_element_type=F32
            )
        fixed_ref[:, at] = total.astype(BF16)
        code = jnp.broadcast_to(code_ref[:, at], (8, tile)).astype(F32)
        payload_ref[:, at] = jnp.concatenate([total, code], axis=0).astype(BF16)
        return carry

    lax.fori_loop(0, count // tile, fix, 0)
    for k, pack_ref in enumerate((pack0, pack1, pack2, pack3, pack4, pack5)):
        packer = ones_where(iota((cap, count), 0) + k * cap == place_ref[...])
        pack_ref[...] = lax.dot_general(
            payload_ref[...], packer, NT, preferred_element_type=F32
        ).astype(BF16)


def correct_call(x, own, near, owner, local, pair, orient, lift, place, code):
    count = x.shape[1]
    cap = count // 16
    faces = owner.shape[2]
    rows = ROWS + 8
    return pl.pallas_call(
        functools.partial(correct_kernel, 512),
        out_shape=[jax.ShapeDtypeStruct((ROWS, count), BF16)]
        + [jax.ShapeDtypeStruct((rows, cap), BF16)] * 6,
        scratch_shapes=[pltpu.VMEM((ROWS, 4 * faces), BF16), pltpu.VMEM((rows, count), BF16)],
        compiler_params=pltpu.CompilerParams(vmem_limit_bytes=56 << 20),
        name="correct",
    )(x, own, *near, owner, local, pair, orient, lift, place, code)


def plan_kernel(move_ref, refine_ref, edge_ref, place_ref, code_ref, state_ref):
    count = move_ref.shape[1]
    block = 256
    cap = count // 16
    before = ones_where(iota((block, block), 0) < iota((block, block), 1))
    seen = jnp.zeros((8, 1), F32)
    which = iota((8, block), 0)
    for b in range(count // block):
        at = slice(b * block, (b + 1) * block)
        move = move_ref[:, at]
        hit = jnp.where(which == move, 1.0, 0.0)
        earlier = dot(hit.astype(BF16), before) + seen
        rank = jnp.sum(hit * earlier, axis=0, keepdims=True).astype(jnp.int32)
        place_ref[:, at] = jnp.where(move < 6, move * cap + rank, 6 * cap)
        seen = seen + jnp.sum(hit, axis=1, keepdims=True)
        code = jnp.where(refine_ref[:, at] == 1, edge_ref[:, at] + 1, 0)
        code_ref[:, at] = code
        state_ref[:, at] = jnp.where(move == 6, code, -1)


def plan_call(move, refine, edge):
    out = jax.ShapeDtypeStruct(move.shape, jnp.int32)
    return pl.pallas_call(plan_kernel, out_shape=[out, out, out], name="plan")(move, refine, edge)


def joined_weights(prolong_ref):
    rows = []
    for c in range(2):
        total = jnp.zeros((PAD, 6 * PAD), F32)
        for e in range(6):
            left = ones_where(iota((PAD, MODES), 0) == iota((PAD, MODES), 1))
            right = ones_where(iota((MODES, 6 * PAD), 0) + e * PAD == iota((MODES, 6 * PAD), 1))
            total += dot(dot(left, prolong_ref[e, c]).astype(BF16), right)
        rows.append(total)
    return jnp.concatenate(rows, axis=0).astype(BF16)


def bisect_tile(weights, parents, state, wide_ref, kids_ref, out_ref, at):
    chunks = state.shape[1] // LANES
    pieces = [slice(i * LANES, (i + 1) * LANES) for i in range(chunks)]
    parents = jnp.where(state >= 0, parents, 0.0)
    for i, piece in enumerate(pieces):
        wide_ref[i, :ROWS, :] = parents[:, piece]
    for f in range(FIELDS):
        modes = jnp.concatenate(
            [wide_ref[i, pl.ds(f, PAD, stride=FIELDS), :] for i in range(chunks)], axis=1
        )
        masked = [jnp.where(state == e + 1, modes, 0.0) for e in range(6)]
        both = dot(weights, jnp.concatenate(masked, axis=0).astype(BF16))
        for i, piece in enumerate(pieces):
            kids_ref[i, pl.ds(f, MODES, stride=FIELDS), :] = both[:MODES, piece]
            kids_ref[i, pl.ds(ROWS + f, MODES, stride=FIELDS), :] = both[PAD : PAD + MODES, piece]
    kids = jnp.concatenate([kids_ref[i] for i in range(chunks)], axis=1)
    out_ref[0, :, at] = jnp.where(state == 0, parents, kids[:ROWS]).astype(BF16)
    out_ref[1, :, at] = kids[ROWS:].astype(BF16)


def home_kernel(tile, fixed_ref, state_ref, prolong_ref, out_ref, wide_ref, kids_ref):
    weights = joined_weights(prolong_ref)
    wide_ref[:, ROWS:, :] = jnp.zeros((tile // LANES, PAD * FIELDS - ROWS, LANES), F32)

    def step(t, carry):
        at = pl.ds(pl.multiple_of(t * tile, tile), tile)
        parents = fixed_ref[:, at].astype(F32)
        bisect_tile(weights, parents, state_ref[:, at], wide_ref, kids_ref, out_ref, at)
        return carry

    lax.fori_loop(0, fixed_ref.shape[1] // tile, step, 0)


def scratch_tiles(tile):
    chunks = tile // LANES
    return [
        pltpu.VMEM((chunks, PAD * FIELDS, LANES), F32),
        pltpu.VMEM((chunks, 2 * ROWS, LANES), F32),
    ]


def home_call(fixed, state, prolong, slots):
    count = fixed.shape[1]
    tile = 512
    return pl.pallas_call(
        functools.partial(home_kernel, tile),
        grid=(1,),
        in_specs=[
            pl.BlockSpec((ROWS, count), lambda i: (0, 0)),
            pl.BlockSpec((1, count), lambda i: (0, 0)),
            pl.BlockSpec(prolong.shape, lambda i: (0, 0, 0, 0)),
        ],
        out_specs=pl.BlockSpec((2, ROWS, count), lambda i: (0, 0, 0)),
        out_shape=jax.ShapeDtypeStruct((2, ROWS, slots), BF16),
        scratch_shapes=scratch_tiles(tile),
        compiler_params=pltpu.CompilerParams(vmem_limit_bytes=48 << 20),
        cost_estimate=pl.CostEstimate(
            flops=2 * 560 * 280 * count, bytes_accessed=6 * ROWS * count, transcendentals=0
        ),
        name="home",
    )(fixed, state, prolong)


def incoming_kernel(
    cap, part0, part1, part2, part3, part4, part5, prolong_ref, kept_ref, out_ref, wide_ref, kids_ref
):
    weights = joined_weights(prolong_ref)
    wide_ref[:, ROWS:, :] = jnp.zeros((cap // LANES, PAD * FIELDS - ROWS, LANES), F32)
    for k, part in enumerate((part0, part1, part2, part3, part4, part5)):
        block = part[...].astype(F32)
        state = block[ROWS : ROWS + 1].astype(jnp.int32)
        at = pl.ds(k * cap, cap)
        bisect_tile(weights, block[:ROWS], state, wide_ref, kids_ref, out_ref, at)


def incoming_call(parts, prolong, kept):
    rows, cap = parts[0].shape
    slots = kept.shape[2]
    return pl.pallas_call(
        functools.partial(incoming_kernel, cap),
        grid=(1,),
        in_specs=[pl.BlockSpec((rows, cap), lambda i: (0, 0))] * 6
        + [
            pl.BlockSpec(prolong.shape, lambda i: (0, 0, 0, 0)),
            pl.BlockSpec(memory_space=pl.ANY),
        ],
        out_specs=pl.BlockSpec(
            (pl.Element(2), pl.Element(ROWS), pl.Element(6 * cap)), lambda i: (0, 0, slots - 6 * cap)
        ),
        out_shape=jax.ShapeDtypeStruct(kept.shape, BF16),
        scratch_shapes=scratch_tiles(cap),
        input_output_aliases={7: 0},
        compiler_params=pltpu.CompilerParams(vmem_limit_bytes=32 << 20),
        name="incoming",
    )(*parts, prolong, kept)


def shards(
    parents,
    refine,
    edge,
    move,
    face_owner,
    face_local,
    face_pair,
    face_orient,
    prolong,
    restrict,
    lift,
):
    count = parents.shape[2]
    slots = count + 6 * (count // 16)
    x = parents.reshape(ROWS, count)
    place, code, state = plan_call(move[None, :], refine[None, :], edge[None, :])
    own = trace_call(x, face_owner, face_local, restrict)
    near = [
        passed_along(own[1], "gx", 1),
        passed_along(own[0], "gx", -1),
        passed_along(own[3], "gz", 1),
        passed_along(own[2], "gz", -1),
    ]
    fixed, *packs = correct_call(
        x, own, near, face_owner, face_local, face_pair, face_orient, lift, place, code
    )
    parts = [passed_along(packs[k], ("gx", "gz"), OFFSETS[k]) for k in range(6)]
    kept = home_call(fixed, state, prolong, slots)
    out = incoming_call(parts, prolong, kept)
    return out.reshape(2, MODES, FIELDS, slots)


def solution(mesh):
    whole = ("gx", "gz")
    side = P(None, whole, None)
    in_specs = (P(None, None, whole), P(whole), P(whole), P(whole), side, side, side, side, P(), P(), P())
    out_specs = P(None, None, None, whole)
    return jax.shard_map(shards, mesh=mesh, in_specs=in_specs, out_specs=out_specs, check_vma=False)
```

```python
import functools

import jax
import jax.numpy as jnp
import numpy as np
from jax import lax
from jax.experimental import pallas as pl
from jax.experimental.pallas import tpu as pltpu
from jax.sharding import PartitionSpec as P

MODES = 35
FMODES = 15
FIELDS = 8
ROWS = MODES * FIELDS
NODE_ROWS = FMODES * FIELDS
PAD = 40
LANES = 128
BUCKET = 512
WINDOW = 256
TILE = 512
LIMIT = 30 << 20
OFFSETS = (1, 2, 3, -1, -2, -3)
F32 = jnp.float32
BF16 = jnp.bfloat16
NT = (((1,), (1,)), ((), ()))


def passed_along(block, axis, distance):
    count = lax.axis_size(axis)
    return lax.ppermute(block, axis, [((i - distance) % count, i) for i in range(count)])


def face_table():
    nodes = [(a, b, 4 - a - b) for a in range(5) for b in range(5 - a)]
    index = {node: place for place, node in enumerate(nodes)}
    orders = [(0, 1, 2), (1, 2, 0), (2, 0, 1), (1, 0, 2), (0, 2, 1), (2, 1, 0)]
    return [[index[n[p[0]], n[p[1]], n[p[2]]] for n in nodes] for p in orders]


def iota(shape, dim):
    return lax.broadcasted_iota(jnp.int32, shape, dim)


def ones_where(mask):
    return jnp.where(mask, 1.0, 0.0).astype(BF16)


def dot(a, b):
    return jnp.dot(a, b, preferred_element_type=F32)


def spread(small, rows, columns):
    height, width = small.shape
    left = ones_where(iota((rows, height), 0) // FIELDS == iota((rows, height), 1))
    right = ones_where(iota((width, columns), 0) == iota((width, columns), 1) // FIELDS)
    full = dot(dot(left, small).astype(BF16), right)
    same = iota((rows, columns), 0) % FIELDS == iota((rows, columns), 1) % FIELDS
    return jnp.where(same, full, 0.0)


VMEM_SPEC = pl.BlockSpec(memory_space=pltpu.VMEM)
SMEM_SPEC = pl.BlockSpec(memory_space=pltpu.SMEM)
HBM_SPEC = pl.BlockSpec(memory_space=pltpu.HBM)


def fetches(sources, targets, sems):
    copies = [pltpu.make_async_copy(a, b, sems.at[i]) for i, (a, b) in enumerate(zip(sources, targets))]
    for copy in copies:
        copy.start()
    return copies


def room(*arrays):
    buffers = [pltpu.VMEM(a.shape, a.dtype) for a in arrays]
    return buffers + [pltpu.SemaphoreType.DMA((len(arrays),))]


def trace_kernel(tile, *refs):
    sources, own_refs, every_ref, held, sems = refs[:4], refs[4:8], refs[8], refs[9:13], refs[13]
    restrict_ref, owner_ref, local_ref, x_ref = held
    copies = fetches(sources, held, sems)
    count = x_ref.shape[1]
    faces = owner_ref.shape[2]
    copies[0].wait()
    spreads = [spread(restrict_ref[:, l, :], NODE_ROWS, ROWS) for l in range(4)]
    every_ref[...] = jnp.concatenate(spreads, axis=0).astype(BF16)
    for copy in copies[1:]:
        copy.wait()
    for s in range(4):

        def step(j, carry, s=s):
            lanes = pl.ds(pl.multiple_of(j * tile, tile), tile)
            owner = owner_ref[s, :, lanes]
            local = local_ref[s, :, lanes]
            onehot = ones_where(iota((count, tile), 0) == owner)
            picked = dot(x_ref[...], onehot).astype(BF16)
            traces = dot(every_ref[...], picked)
            chosen = traces[:NODE_ROWS]
            for l in range(1, 4):
                chosen = jnp.where(local == l, traces[l * NODE_ROWS : (l + 1) * NODE_ROWS], chosen)
            own_refs[s][:, lanes] = chosen.astype(BF16)
            return carry

        lax.fori_loop(0, faces // tile, step, 0)


def trace_call(x, owner, local, restrict):
    faces = owner.shape[2]
    return pl.pallas_call(
        functools.partial(trace_kernel, 512),
        in_specs=[HBM_SPEC] * 4,
        out_specs=[VMEM_SPEC] * 4,
        out_shape=[jax.ShapeDtypeStruct((NODE_ROWS, faces), BF16)] * 4,
        scratch_shapes=[pltpu.VMEM((4 * NODE_ROWS, ROWS), BF16)] + room(restrict, owner, local, x),
        compiler_params=pltpu.CompilerParams(vmem_limit_bytes=LIMIT),
        cost_estimate=pl.CostEstimate(flops=10**10, bytes_accessed=10**7, transcendentals=0),
        name="trace",
    )(*[pltpu.with_memory_space_constraint(a, pltpu.HBM) for a in (restrict, owner, local, x)])


def rank_moves(move_ref, refine_ref, edge_ref, place_ref, code_ref, state_ref):
    count = move_ref.shape[1]
    block = 256
    cap = count // 16
    before = ones_where(iota((block, block), 0) < iota((block, block), 1))
    seen = jnp.zeros((8, 1), F32)
    which = iota((8, block), 0)
    for b in range(count // block):
        at = slice(b * block, (b + 1) * block)
        move = move_ref[:, at]
        hit = jnp.where(which == move, 1.0, 0.0)
        earlier = dot(hit.astype(BF16), before) + seen
        rank = jnp.sum(hit * earlier, axis=0, keepdims=True).astype(jnp.int32)
        place_ref[:, at] = jnp.where(move < 6, move * cap + rank, 6 * cap)
        seen = seen + jnp.sum(hit, axis=1, keepdims=True)
        code = jnp.where(refine_ref[:, at] == 1, edge_ref[:, at] + 1, 0)
        code_ref[:, at] = code
        state_ref[:, at] = jnp.where(move == 6, code, -1)


def plan_kernel(*refs):
    own_refs, sources, held, sems = refs[:4], refs[4:11], refs[17:24], refs[24]
    own_ref, meta_ref, table_ref, place_ref, code_ref, state_ref = refs[11:17]
    owner_ref, local_ref, pair_ref, orient_ref, move_ref, refine_ref, edge_ref = held
    for copy in fetches(sources, held, sems):
        copy.wait()
    rank_moves(move_ref, refine_ref, edge_ref, place_ref, code_ref, state_ref)
    faces = owner_ref.shape[2]
    block = 256
    before = ones_where(iota((block, block), 0) < iota((block, block), 1))
    eight = iota((8, faces), 0)
    buckets = [owner_ref[s] // BUCKET for s in range(4)]
    hits = jnp.concatenate([jnp.where(eight == b, 1.0, 0.0) for b in buckets], axis=0)
    smaller = jnp.concatenate([jnp.where(b < eight, 1.0, 0.0) for b in buckets], axis=0)
    start = jnp.sum(smaller, axis=1, keepdims=True)
    end = start + jnp.sum(hits, axis=1, keepdims=True)
    first = start.astype(jnp.int32)
    last = end.astype(jnp.int32)
    begin = jnp.minimum(first // LANES * LANES, faces - LANES)
    trips = (last - begin + WINDOW - 1) // WINDOW
    longest = jnp.maximum(
        jnp.maximum(trips[0:8], trips[8:16]), jnp.maximum(trips[16:24], trips[24:32])
    )
    longest = jnp.concatenate([longest] * 4, axis=0)
    lane = iota((32, LANES), 1)
    table_ref[...] = jnp.where(lane == 0, begin, jnp.where(lane == 1, trips, longest))
    seen = start
    places = []
    for b in range(faces // block):
        part = hits[:, b * block : (b + 1) * block]
        places.append(part * (dot(part.astype(BF16), before) + seen))
        seen = seen + jnp.sum(part, axis=1, keepdims=True)
    places = jnp.concatenate(places, axis=1)
    meta_ref[...] = jnp.full(meta_ref.shape, -1, jnp.int32)
    for s in range(4):
        spot = jnp.sum(places[8 * s : 8 * s + 8], axis=0, keepdims=True).astype(jnp.int32)
        order = ones_where(iota((faces, faces), 0) == spot)
        owner, pair = owner_ref[s], pair_ref[s]
        values = (owner // 256, owner % 256, local_ref[s], pair // 256, pair % 256, orient_ref[s])
        small = jnp.zeros((8, faces), jnp.int32)
        for row, value in enumerate(values):
            small = jnp.where(eight == row, value, small)
        both = jnp.concatenate([own_refs[s][...].astype(F32), small.astype(F32)], axis=0)
        moved = lax.dot_general(both.astype(BF16), order, NT, preferred_element_type=F32)
        own_ref[s] = moved[:NODE_ROWS].astype(BF16)
        got = moved[NODE_ROWS:].astype(jnp.int32)
        rows = (got[0:1] * 256 + got[1:2], got[2:3], got[3:4] * 256 + got[4:5], got[5:6])
        meta = jnp.zeros((8, faces), jnp.int32)
        for row, value in enumerate(rows):
            meta = jnp.where(eight == row, value, meta)
        meta_ref[s, :, :faces] = meta


def plan_call(owns, *rest):
    faces = rest[0].shape[2]
    flat = jax.ShapeDtypeStruct(rest[-1].shape, jnp.int32)
    return pl.pallas_call(
        plan_kernel,
        in_specs=[VMEM_SPEC] * 4 + [HBM_SPEC] * 7,
        out_specs=[VMEM_SPEC] * 6,
        out_shape=[
            jax.ShapeDtypeStruct((4, NODE_ROWS, faces), BF16),
            jax.ShapeDtypeStruct((4, 8, faces + LANES), jnp.int32),
            jax.ShapeDtypeStruct((32, LANES), jnp.int32),
            flat,
            flat,
            flat,
        ],
        scratch_shapes=room(*rest),
        compiler_params=pltpu.CompilerParams(vmem_limit_bytes=LIMIT),
        cost_estimate=pl.CostEstimate(flops=5 * 10**9, bytes_accessed=4 * 10**6, transcendentals=0),
        name="plan",
    )(*owns, *rest)


def correct_kernel(tile, *refs):
    lift_hbm, x_hbm, own_ref = refs[:3]
    near_refs = refs[3:7]
    meta_ref, table_ref, place_ref, code_ref, fixed_ref = refs[7:12]
    pack_refs = refs[12:18]
    lifted_ref, payload_ref, total_ref, lift_ref, x_ref, sems = refs[18:]
    copies = fetches((lift_hbm, x_hbm), (lift_ref, x_ref), sems)
    count = x_ref.shape[1]
    faces = own_ref.shape[2]
    cap = pack_refs[0].shape[1]
    table = face_table()
    copies[0].wait()
    raised = [spread(lift_ref[:, l, :].astype(BF16), NODE_ROWS, ROWS) for l in range(4)]
    raised = jnp.concatenate(raised, axis=0).T.astype(BF16)

    def jumps(j, carry):
        lanes = pl.ds(pl.multiple_of(j * tile, tile), tile)
        for s in range(4):
            local = meta_ref[s, 1:2, lanes]
            pair = meta_ref[s, 2:3, lanes]
            orient = meta_ref[s, 3:4, lanes]
            matcher = ones_where(iota((faces, tile), 0) == pair)
            paired = dot(near_refs[s][...], matcher)
            own = own_ref[s, :, lanes].astype(F32)
            jump = []
            for n in range(FMODES):
                best = paired[table[0][n] * FIELDS : (table[0][n] + 1) * FIELDS]
                for o in range(1, 6):
                    if table[o][n] != table[0][n]:
                        other = paired[table[o][n] * FIELDS : (table[o][n] + 1) * FIELDS]
                        best = jnp.where(orient == o, other, best)
                jump.append(0.5 * (best - own[n * FIELDS : (n + 1) * FIELDS]))
            jump = jnp.concatenate(jump, axis=0)
            split = jnp.concatenate([jnp.where(local == l, jump, 0.0) for l in range(4)], axis=0)
            lifted_ref[s, :, lanes] = dot(raised, split.astype(BF16)).astype(BF16)
        return carry

    for s in range(4):
        lifted_ref[s, :, faces:] = jnp.zeros((ROWS, LANES), BF16)
    lax.fori_loop(0, faces // tile, jumps, 0)
    copies[1].wait()

    def fix(t, carry):
        at = pl.ds(pl.multiple_of(t * BUCKET, BUCKET), BUCKET)
        parent = iota((BUCKET, WINDOW), 0) + t * BUCKET

        def window(s, i):
            begin = table_ref[8 * s + t, 0] + i * WINDOW
            lanes = pl.ds(pl.multiple_of(begin, LANES), WINDOW)
            return lifted_ref[s, :, lanes], ones_where(parent == meta_ref[s, 0:1, lanes])

        both = [window(s, 0) for s in range(4)]
        total = x_ref[:, at].astype(F32) + lax.dot_general(
            jnp.concatenate([a for a, _ in both], axis=1),
            jnp.concatenate([b for _, b in both], axis=1),
            NT,
            preferred_element_type=F32,
        )
        total_ref[...] = total

        @pl.when(table_ref[t, 2] > 1)
        def _():
            for s in range(4):

                def more(i, carry, s=s):
                    a, b = window(s, i)
                    total_ref[...] += lax.dot_general(a, b, NT, preferred_element_type=F32)
                    return carry

                lax.fori_loop(1, table_ref[8 * s + t, 1], more, 0)

        total = total_ref[...]
        fixed_ref[:, at] = total.astype(BF16)
        code = jnp.broadcast_to(code_ref[:, at], (8, BUCKET)).astype(F32)
        payload_ref[:, at] = jnp.concatenate([total, code], axis=0).astype(BF16)
        return carry

    lax.fori_loop(0, count // BUCKET, fix, 0)
    for k, pack_ref in enumerate(pack_refs):
        packer = ones_where(iota((cap, count), 0) + k * cap == place_ref[...])
        pack_ref[...] = lax.dot_general(
            payload_ref[...], packer, NT, preferred_element_type=F32
        ).astype(BF16)


def correct_call(x, own, near, meta, table, lift, place, code):
    count = x.shape[1]
    cap = count // 16
    faces = own.shape[2]
    rows = ROWS + 8
    return pl.pallas_call(
        functools.partial(correct_kernel, 512),
        in_specs=[HBM_SPEC] * 2 + [VMEM_SPEC] * 6 + [SMEM_SPEC] + [VMEM_SPEC] * 2,
        out_specs=[VMEM_SPEC] * 7,
        out_shape=[jax.ShapeDtypeStruct((ROWS, count), BF16)]
        + [jax.ShapeDtypeStruct((rows, cap), BF16)] * 6,
        scratch_shapes=[
            pltpu.VMEM((4, ROWS, faces + LANES), BF16),
            pltpu.VMEM((rows, count), BF16),
            pltpu.VMEM((ROWS, BUCKET), F32),
        ]
        + room(lift, x),
        compiler_params=pltpu.CompilerParams(vmem_limit_bytes=LIMIT),
        cost_estimate=pl.CostEstimate(flops=10**10, bytes_accessed=10**7, transcendentals=0),
        name="correct",
    )(lift, x, own, *near, meta, table, place, code)


def joined_weights(prolong_ref):
    rows = []
    for c in range(2):
        total = jnp.zeros((PAD, 6 * PAD), F32)
        for e in range(6):
            left = ones_where(iota((PAD, MODES), 0) == iota((PAD, MODES), 1))
            right = ones_where(iota((MODES, 6 * PAD), 0) + e * PAD == iota((MODES, 6 * PAD), 1))
            total += dot(dot(left, prolong_ref[e, :, c, :]).astype(BF16), right)
        rows.append(total)
    return jnp.concatenate(rows, axis=0).astype(BF16)


def bisect_tile(weights, parents, state, wide_ref, kids_ref, put):
    chunks = state.shape[1] // LANES
    pieces = [slice(i * LANES, (i + 1) * LANES) for i in range(chunks)]
    parents = jnp.where(state >= 0, parents, 0.0)
    for i, piece in enumerate(pieces):
        wide_ref[i, :ROWS, :] = parents[:, piece]
    for f in range(FIELDS):
        modes = jnp.concatenate(
            [wide_ref[i, pl.ds(f, PAD, stride=FIELDS), :] for i in range(chunks)], axis=1
        )
        masked = [jnp.where(state == e + 1, modes, 0.0) for e in range(6)]
        both = dot(weights, jnp.concatenate(masked, axis=0).astype(BF16))
        for i, piece in enumerate(pieces):
            kids_ref[i, pl.ds(f, MODES, stride=FIELDS), :] = both[:MODES, piece]
            kids_ref[i, pl.ds(ROWS + f, MODES, stride=FIELDS), :] = both[PAD : PAD + MODES, piece]
    kids = jnp.concatenate([kids_ref[i] for i in range(chunks)], axis=1)
    put(0, jnp.where(state == 0, parents, kids[:ROWS]).astype(BF16))
    put(1, kids[ROWS:].astype(BF16))


def scratch_tiles():
    return [
        pltpu.VMEM((2 * MODES + 2 * (PAD - MODES), 6 * PAD), BF16),
        pltpu.VMEM((TILE // LANES, PAD * FIELDS, LANES), F32),
        pltpu.VMEM((TILE // LANES, 2 * ROWS, LANES), F32),
    ]


def clear(wide_ref):
    wide_ref[:, ROWS:, :] = jnp.zeros((TILE // LANES, PAD * FIELDS - ROWS, LANES), F32)


def home_kernel(fixed_ref, state_ref, prolong_ref, out_ref, weights_ref, wide_ref, kids_ref):
    t = pl.program_id(0)

    @pl.when(t == 0)
    def _():
        weights_ref[...] = joined_weights(prolong_ref)
        clear(wide_ref)

    at = pl.ds(pl.multiple_of(t * TILE, TILE), TILE)

    def put(child, value):
        out_ref[child] = value

    parents = fixed_ref[:, at].astype(F32)
    bisect_tile(weights_ref[...], parents, state_ref[:, at], wide_ref, kids_ref, put)


def home_call(fixed, state, prolong, slots):
    count = fixed.shape[1]
    return pl.pallas_call(
        home_kernel,
        grid=(count // TILE,),
        in_specs=[VMEM_SPEC, VMEM_SPEC, VMEM_SPEC],
        out_specs=pl.BlockSpec((2, ROWS, TILE), lambda i: (0, 0, i)),
        out_shape=jax.ShapeDtypeStruct((2, ROWS, slots), BF16),
        scratch_shapes=scratch_tiles(),
        compiler_params=pltpu.CompilerParams(vmem_limit_bytes=LIMIT),
        cost_estimate=pl.CostEstimate(
            flops=2 * 560 * 280 * count, bytes_accessed=6 * ROWS * count, transcendentals=0
        ),
        name="home",
    )(fixed, state, prolong)


def incoming_kernel(*refs):
    parts, prolong_ref, out_hbm = refs[:6], refs[6], refs[8]
    weights_ref, wide_ref, kids_ref, out_ref, sems = refs[9:]
    cap = parts[0].shape[1]
    first = out_hbm.shape[2] - 6 * cap
    weights_ref[...] = joined_weights(prolong_ref)
    clear(wide_ref)
    copies = []
    for k in range(3):
        block = jnp.concatenate([parts[2 * k][...], parts[2 * k + 1][...]], axis=1).astype(F32)
        state = block[ROWS : ROWS + 1].astype(jnp.int32)

        def put(child, value, k=k):
            out_ref[k, child] = value

        bisect_tile(weights_ref[...], block[:ROWS], state, wide_ref, kids_ref, put)
        target = out_hbm.at[:, :, pl.ds(first + k * TILE, TILE)]
        copies.append(pltpu.make_async_copy(out_ref.at[k], target, sems.at[k]))
        copies[-1].start()
    for copy in copies:
        copy.wait()


def incoming_call(parts, prolong, kept):
    return pl.pallas_call(
        incoming_kernel,
        in_specs=[VMEM_SPEC] * 7 + [HBM_SPEC],
        out_specs=HBM_SPEC,
        out_shape=jax.ShapeDtypeStruct(kept.shape, BF16),
        scratch_shapes=scratch_tiles()
        + [pltpu.VMEM((3, 2, ROWS, TILE), BF16), pltpu.SemaphoreType.DMA((3,))],
        input_output_aliases={7: 0},
        compiler_params=pltpu.CompilerParams(vmem_limit_bytes=LIMIT),
        name="incoming",
    )(*parts, prolong, kept)


def shards(
    parents,
    refine,
    edge,
    move,
    face_owner,
    face_local,
    face_pair,
    face_orient,
    prolong,
    restrict,
    lift,
):
    count = parents.shape[2]
    slots = count + 6 * (count // 16)
    x = parents.reshape(ROWS, count)
    prolong = prolong.transpose(0, 2, 1, 3)
    owns = trace_call(x, face_owner, face_local, restrict.transpose(1, 0, 2))
    near = [
        passed_along(owns[1], "gx", 1),
        passed_along(owns[0], "gx", -1),
        passed_along(owns[3], "gz", 1),
        passed_along(owns[2], "gz", -1),
    ]
    own, meta, table, place, code, state = plan_call(
        owns,
        face_owner,
        face_local,
        face_pair,
        face_orient,
        move[None, :],
        refine[None, :],
        edge[None, :],
    )
    fixed, *packs = correct_call(
        x, own, near, meta, table, lift.transpose(2, 0, 1), place, code
    )
    parts = [passed_along(packs[k], ("gx", "gz"), OFFSETS[k]) for k in range(6)]
    kept = home_call(fixed, state, prolong, slots)
    out = incoming_call(parts, prolong, kept)
    return out.reshape(2, MODES, FIELDS, slots)


def solution(mesh):
    whole = ("gx", "gz")
    side = P(None, whole, None)
    in_specs = (P(None, None, whole), P(whole), P(whole), P(whole), side, side, side, side, P(), P(), P())
    out_specs = P(None, None, None, whole)
    return jax.shard_map(shards, mesh=mesh, in_specs=in_specs, out_specs=out_specs, check_vma=False)
```

```python
import functools

import jax
import jax.numpy as jnp
from jax import lax
from jax.experimental import pallas as pl
from jax.experimental.pallas import tpu as pltpu
from jax.sharding import PartitionSpec as P

MODES = 35
FMODES = 15
FIELDS = 8
ROWS = MODES * FIELDS
NODE_ROWS = FMODES * FIELDS
PAD = 40
LANES = 128
BUCKET = 512
WINDOW = 256
TILE = 512
LIMIT = 30 << 20
OFFSETS = (1, 2, 3, -1, -2, -3)
F32 = jnp.float32
BF16 = jnp.bfloat16
NT = (((1,), (1,)), ((), ()))


def passed_along(block, axis, distance):
    count = lax.axis_size(axis)
    return lax.ppermute(block, axis, [((i - distance) % count, i) for i in range(count)])


def face_table():
    nodes = [(a, b, 4 - a - b) for a in range(5) for b in range(5 - a)]
    index = {node: place for place, node in enumerate(nodes)}
    orders = [(0, 1, 2), (1, 2, 0), (2, 0, 1), (1, 0, 2), (0, 2, 1), (2, 1, 0)]
    return [[index[n[p[0]], n[p[1]], n[p[2]]] for n in nodes] for p in orders]


def iota(shape, dim):
    return lax.broadcasted_iota(jnp.int32, shape, dim)


def ones_where(mask):
    return jnp.where(mask, 1.0, 0.0).astype(BF16)


def match(rows, row):
    shape = (rows, row.shape[1])
    lines = lax.broadcasted_iota(jnp.int16, shape, 0)
    same = lines == jnp.broadcast_to(row.astype(jnp.int16), shape)
    return jnp.where(same, jnp.array(1, BF16), jnp.array(0, BF16))


def dot(a, b):
    return jnp.dot(a, b, preferred_element_type=F32)


def spread(small, rows, columns):
    height, width = small.shape
    left = ones_where(iota((rows, height), 0) // FIELDS == iota((rows, height), 1))
    right = ones_where(iota((width, columns), 0) == iota((width, columns), 1) // FIELDS)
    full = dot(dot(left, small).astype(BF16), right)
    same = iota((rows, columns), 0) % FIELDS == iota((rows, columns), 1) % FIELDS
    return jnp.where(same, full, 0.0)


VMEM_SPEC = pl.BlockSpec(memory_space=pltpu.VMEM)
SMEM_SPEC = pl.BlockSpec(memory_space=pltpu.SMEM)
HBM_SPEC = pl.BlockSpec(memory_space=pltpu.HBM)


def fetches(sources, targets, sems):
    copies = [pltpu.make_async_copy(a, b, sems.at[i]) for i, (a, b) in enumerate(zip(sources, targets))]
    for copy in copies:
        copy.start()
    return copies


def room(*arrays):
    buffers = [pltpu.VMEM(a.shape, a.dtype) for a in arrays]
    return buffers + [pltpu.SemaphoreType.DMA((len(arrays),))]


def trace_kernel(tile, *refs):
    sources, own_refs, every_ref, held, sems = refs[:4], refs[4:8], refs[8], refs[9:13], refs[13]
    restrict_ref, owner_ref, local_ref, x_ref = held
    copies = fetches(sources, held, sems)
    count = x_ref.shape[1]
    faces = owner_ref.shape[2]
    copies[0].wait()
    spreads = [spread(restrict_ref[:, l, :], NODE_ROWS, ROWS) for l in range(4)]
    every_ref[...] = jnp.concatenate(spreads, axis=0).astype(BF16)
    for copy in copies[1:]:
        copy.wait()
    for s in range(4):

        def step(j, carry, s=s):
            lanes = pl.ds(pl.multiple_of(j * tile, tile), tile)
            owner = owner_ref[s, :, lanes]
            local = local_ref[s, :, lanes]
            onehot = match(count, owner)
            picked = dot(x_ref[...], onehot).astype(BF16)
            traces = dot(every_ref[...], picked)
            chosen = traces[:NODE_ROWS]
            for l in range(1, 4):
                chosen = jnp.where(local == l, traces[l * NODE_ROWS : (l + 1) * NODE_ROWS], chosen)
            own_refs[s][:, lanes] = chosen.astype(BF16)
            return carry

        lax.fori_loop(0, faces // tile, step, 0)


def trace_call(x, owner, local, restrict):
    faces = owner.shape[2]
    return pl.pallas_call(
        functools.partial(trace_kernel, 1024),
        in_specs=[HBM_SPEC] * 4,
        out_specs=[VMEM_SPEC] * 4,
        out_shape=[jax.ShapeDtypeStruct((NODE_ROWS, faces), BF16)] * 4,
        scratch_shapes=[pltpu.VMEM((4 * NODE_ROWS, ROWS), BF16)] + room(restrict, owner, local, x),
        compiler_params=pltpu.CompilerParams(vmem_limit_bytes=LIMIT),
        cost_estimate=pl.CostEstimate(flops=10**10, bytes_accessed=10**7, transcendentals=0),
        name="trace",
    )(*[pltpu.with_memory_space_constraint(a, pltpu.HBM) for a in (restrict, owner, local, x)])


def rank_moves(move_ref, refine_ref, edge_ref, place_ref, code_ref, state_ref):
    count = move_ref.shape[1]
    block = 256
    cap = count // 16
    before = ones_where(iota((block, block), 0) < iota((block, block), 1))
    seen = jnp.zeros((8, 1), F32)
    which = iota((8, block), 0)
    for b in range(count // block):
        at = slice(b * block, (b + 1) * block)
        move = move_ref[:, at]
        hit = jnp.where(which == move, 1.0, 0.0)
        earlier = dot(hit.astype(BF16), before) + seen
        rank = jnp.sum(hit * earlier, axis=0, keepdims=True).astype(jnp.int32)
        place_ref[:, at] = jnp.where(move < 6, move * cap + rank, 6 * cap)
        seen = seen + jnp.sum(hit, axis=1, keepdims=True)
        code = jnp.where(refine_ref[:, at] == 1, edge_ref[:, at] + 1, 0)
        code_ref[:, at] = code
        state_ref[:, at] = jnp.where(move == 6, code, -1)


def plan_kernel(*refs):
    own_refs, sources, held, sems = refs[:4], refs[4:12], refs[19:27], refs[27]
    own_ref, meta_ref, table_ref, raised_ref, place_ref, code_ref, state_ref = refs[12:19]
    owner_ref, local_ref, pair_ref, orient_ref, lift_ref, move_ref, refine_ref, edge_ref = held
    for copy in fetches(sources, held, sems):
        copy.wait()
    rank_moves(move_ref, refine_ref, edge_ref, place_ref, code_ref, state_ref)
    raised = [spread(lift_ref[:, l, :].astype(BF16), NODE_ROWS, ROWS) for l in range(4)]
    raised_ref[...] = jnp.concatenate(raised, axis=0).T.astype(BF16)
    faces = owner_ref.shape[2]
    block = 256
    before = ones_where(iota((block, block), 0) < iota((block, block), 1))
    eight = iota((8, faces), 0)
    buckets = [owner_ref[s] // BUCKET for s in range(4)]
    hits = jnp.concatenate([jnp.where(eight == b, 1.0, 0.0) for b in buckets], axis=0)
    smaller = jnp.concatenate([jnp.where(b < eight, 1.0, 0.0) for b in buckets], axis=0)
    start = jnp.sum(smaller, axis=1, keepdims=True)
    end = start + jnp.sum(hits, axis=1, keepdims=True)
    first = start.astype(jnp.int32)
    last = end.astype(jnp.int32)
    begin = jnp.minimum(first // LANES * LANES, faces - LANES)
    trips = (last - begin + WINDOW - 1) // WINDOW
    longest = jnp.maximum(
        jnp.maximum(trips[0:8], trips[8:16]), jnp.maximum(trips[16:24], trips[24:32])
    )
    longest = jnp.concatenate([longest] * 4, axis=0)
    lane = iota((32, LANES), 1)
    table_ref[...] = jnp.where(lane == 0, begin, jnp.where(lane == 1, trips, longest))
    seen = start
    places = []
    for b in range(faces // block):
        part = hits[:, b * block : (b + 1) * block]
        places.append(part * (dot(part.astype(BF16), before) + seen))
        seen = seen + jnp.sum(part, axis=1, keepdims=True)
    places = jnp.concatenate(places, axis=1)
    meta_ref[...] = jnp.full(meta_ref.shape, -1, jnp.int32)
    for s in range(4):
        spot = jnp.sum(places[8 * s : 8 * s + 8], axis=0, keepdims=True).astype(jnp.int32)
        order = match(faces, spot)
        owner, pair = owner_ref[s], pair_ref[s]
        values = (owner // 256, owner % 256, local_ref[s], pair // 256, pair % 256, orient_ref[s])
        small = jnp.zeros((8, faces), jnp.int32)
        for row, value in enumerate(values):
            small = jnp.where(eight == row, value, small)
        both = jnp.concatenate([own_refs[s][...].astype(F32), small.astype(F32)], axis=0)
        moved = lax.dot_general(both.astype(BF16), order, NT, preferred_element_type=F32)
        own_ref[s] = moved[:NODE_ROWS].astype(BF16)
        got = moved[NODE_ROWS:].astype(jnp.int32)
        rows = (got[0:1] * 256 + got[1:2], got[2:3], got[3:4] * 256 + got[4:5], got[5:6])
        meta = jnp.zeros((8, faces), jnp.int32)
        for row, value in enumerate(rows):
            meta = jnp.where(eight == row, value, meta)
        meta_ref[s, :, :faces] = meta


def plan_call(owns, *rest):
    faces = rest[0].shape[2]
    flat = jax.ShapeDtypeStruct(rest[-1].shape, jnp.int32)
    return pl.pallas_call(
        plan_kernel,
        in_specs=[VMEM_SPEC] * 4 + [HBM_SPEC] * 8,
        out_specs=[VMEM_SPEC] * 7,
        out_shape=[
            jax.ShapeDtypeStruct((4, NODE_ROWS, faces), BF16),
            jax.ShapeDtypeStruct((4, 8, faces + LANES), jnp.int32),
            jax.ShapeDtypeStruct((32, LANES), jnp.int32),
            jax.ShapeDtypeStruct((ROWS, 4 * NODE_ROWS), BF16),
            flat,
            flat,
            flat,
        ],
        scratch_shapes=room(*rest),
        compiler_params=pltpu.CompilerParams(vmem_limit_bytes=LIMIT),
        cost_estimate=pl.CostEstimate(flops=5 * 10**9, bytes_accessed=4 * 10**6, transcendentals=0),
        name="plan",
    )(*owns, *rest)


def correct_kernel(tile, *refs):
    raised_ref, x_hbm, own_ref = refs[:3]
    near_refs = refs[3:7]
    meta_ref, table_ref, place_ref, code_ref, fixed_ref = refs[7:12]
    pack_refs = refs[12:18]
    lifted_ref, payload_ref, total_ref, x_ref, sems = refs[18:]
    copies = fetches((x_hbm,), (x_ref,), sems)
    count = x_ref.shape[1]
    faces = own_ref.shape[2]
    cap = pack_refs[0].shape[1]
    table = face_table()

    def jumps(j, carry):
        lanes = pl.ds(pl.multiple_of(j * tile, tile), tile)
        for s in range(4):
            local = meta_ref[s, 1:2, lanes]
            pair = meta_ref[s, 2:3, lanes]
            orient = meta_ref[s, 3:4, lanes]
            matcher = match(faces, pair)
            paired = dot(near_refs[s][...], matcher)
            own = own_ref[s, :, lanes].astype(F32)
            jump = []
            for n in range(FMODES):
                best = paired[table[0][n] * FIELDS : (table[0][n] + 1) * FIELDS]
                for o in range(1, 6):
                    if table[o][n] != table[0][n]:
                        other = paired[table[o][n] * FIELDS : (table[o][n] + 1) * FIELDS]
                        best = jnp.where(orient == o, other, best)
                jump.append(0.5 * (best - own[n * FIELDS : (n + 1) * FIELDS]))
            jump = jnp.concatenate(jump, axis=0)
            split = jnp.concatenate([jnp.where(local == l, jump, 0.0) for l in range(4)], axis=0)
            lifted_ref[s, :, lanes] = dot(raised_ref[...], split.astype(BF16)).astype(BF16)
        return carry

    for s in range(4):
        lifted_ref[s, :, faces:] = jnp.zeros((ROWS, LANES), BF16)
    lax.fori_loop(0, faces // tile, jumps, 0)
    copies[0].wait()

    def fix(t, carry):
        at = pl.ds(pl.multiple_of(t * BUCKET, BUCKET), BUCKET)

        def window(s, i):
            begin = table_ref[8 * s + t, 0] + i * WINDOW
            lanes = pl.ds(pl.multiple_of(begin, LANES), WINDOW)
            return lifted_ref[s, :, lanes], match(BUCKET, meta_ref[s, 0:1, lanes] - t * BUCKET)

        both = [window(s, 0) for s in range(4)]
        total = x_ref[:, at].astype(F32) + lax.dot_general(
            jnp.concatenate([a for a, _ in both], axis=1),
            jnp.concatenate([b for _, b in both], axis=1),
            NT,
            preferred_element_type=F32,
        )
        total_ref[...] = total

        @pl.when(table_ref[t, 2] > 1)
        def _():
            for s in range(4):

                def more(i, carry, s=s):
                    a, b = window(s, i)
                    total_ref[...] += lax.dot_general(a, b, NT, preferred_element_type=F32)
                    return carry

                lax.fori_loop(1, table_ref[8 * s + t, 1], more, 0)

        total = total_ref[...]
        fixed_ref[:, at] = total.astype(BF16)
        code = jnp.broadcast_to(code_ref[:, at], (8, BUCKET)).astype(F32)
        payload_ref[:, at] = jnp.concatenate([total, code], axis=0).astype(BF16)
        return carry

    lax.fori_loop(0, count // BUCKET, fix, 0)
    for k, pack_ref in enumerate(pack_refs):
        packer = match(cap, place_ref[...] - k * cap)
        pack_ref[...] = lax.dot_general(
            payload_ref[...], packer, NT, preferred_element_type=F32
        ).astype(BF16)


def correct_call(x, own, near, meta, table, raised, place, code):
    count = x.shape[1]
    cap = count // 16
    faces = own.shape[2]
    rows = ROWS + 8
    return pl.pallas_call(
        functools.partial(correct_kernel, 512),
        in_specs=[VMEM_SPEC, HBM_SPEC] + [VMEM_SPEC] * 6 + [SMEM_SPEC] + [VMEM_SPEC] * 2,
        out_specs=[VMEM_SPEC] * 7,
        out_shape=[jax.ShapeDtypeStruct((ROWS, count), BF16)]
        + [jax.ShapeDtypeStruct((rows, cap), BF16)] * 6,
        scratch_shapes=[
            pltpu.VMEM((4, ROWS, faces + LANES), BF16),
            pltpu.VMEM((rows, count), BF16),
            pltpu.VMEM((ROWS, BUCKET), F32),
        ]
        + room(x),
        compiler_params=pltpu.CompilerParams(vmem_limit_bytes=LIMIT),
        cost_estimate=pl.CostEstimate(flops=10**10, bytes_accessed=10**7, transcendentals=0),
        name="correct",
    )(raised, x, own, *near, meta, table, place, code)


def joined_weights(prolong_ref):
    rows = []
    for c in range(2):
        total = jnp.zeros((PAD, 6 * PAD), F32)
        for e in range(6):
            left = ones_where(iota((PAD, MODES), 0) == iota((PAD, MODES), 1))
            right = ones_where(iota((MODES, 6 * PAD), 0) + e * PAD == iota((MODES, 6 * PAD), 1))
            total += dot(dot(left, prolong_ref[e, :, c, :]).astype(BF16), right)
        rows.append(total)
    return jnp.concatenate(rows, axis=0).astype(BF16)


def bisect_tile(weights, parents, state, wide_ref, kids_ref, put):
    chunks = state.shape[1] // LANES
    pieces = [slice(i * LANES, (i + 1) * LANES) for i in range(chunks)]
    parents = jnp.where(state >= 0, parents, 0.0)
    shape = (2 * PAD, state.shape[1])
    second = (iota(shape, 0) // PAD).astype(jnp.int16)
    cut = jnp.broadcast_to((state - 1).astype(jnp.int16), shape) - second
    for i, piece in enumerate(pieces):
        wide_ref[i, :ROWS, :] = parents[:, piece]
    for f in range(FIELDS):
        modes = jnp.concatenate(
            [wide_ref[i, pl.ds(f, PAD, stride=FIELDS), :] for i in range(chunks)], axis=1
        )
        twice = jnp.concatenate([modes, modes], axis=0).astype(BF16)
        masked = [jnp.where(cut == 2 * i, twice, jnp.array(0, BF16)) for i in range(3)]
        both = dot(weights, jnp.concatenate(masked, axis=0))
        for i, piece in enumerate(pieces):
            kids_ref[i, pl.ds(f, MODES, stride=FIELDS), :] = both[:MODES, piece]
            kids_ref[i, pl.ds(ROWS + f, MODES, stride=FIELDS), :] = both[PAD : PAD + MODES, piece]
    kids = jnp.concatenate([kids_ref[i] for i in range(chunks)], axis=1)
    put(0, jnp.where(state == 0, parents, kids[:ROWS]).astype(BF16))
    put(1, kids[ROWS:].astype(BF16))


def scratch_tiles():
    return [
        pltpu.VMEM((TILE // LANES, PAD * FIELDS, LANES), F32),
        pltpu.VMEM((TILE // LANES, 2 * ROWS, LANES), F32),
    ]


def clear(wide_ref):
    wide_ref[:, ROWS:, :] = jnp.zeros((TILE // LANES, PAD * FIELDS - ROWS, LANES), F32)


def home_kernel(fixed_ref, state_ref, prolong_ref, out_ref, weights_ref, wide_ref, kids_ref):
    t = pl.program_id(0)

    @pl.when(t == 0)
    def _():
        weights_ref[...] = joined_weights(prolong_ref)
        clear(wide_ref)

    at = pl.ds(pl.multiple_of(t * TILE, TILE), TILE)

    def put(child, value):
        out_ref[child] = value

    parents = fixed_ref[:, at].astype(F32)
    bisect_tile(weights_ref[...], parents, state_ref[:, at], wide_ref, kids_ref, put)


def home_call(fixed, state, prolong, slots):
    count = fixed.shape[1]
    return pl.pallas_call(
        home_kernel,
        grid=(count // TILE,),
        in_specs=[VMEM_SPEC, VMEM_SPEC, VMEM_SPEC],
        out_specs=[
            pl.BlockSpec((2, ROWS, TILE), lambda i: (0, 0, i)),
            pl.BlockSpec((2 * PAD, 6 * PAD), lambda i: (0, 0)),
        ],
        out_shape=[
            jax.ShapeDtypeStruct((2, ROWS, slots), BF16),
            jax.ShapeDtypeStruct((2 * PAD, 6 * PAD), BF16),
        ],
        scratch_shapes=scratch_tiles(),
        compiler_params=pltpu.CompilerParams(vmem_limit_bytes=LIMIT),
        cost_estimate=pl.CostEstimate(
            flops=2 * 560 * 280 * count, bytes_accessed=6 * ROWS * count, transcendentals=0
        ),
        name="home",
    )(fixed, state, prolong)


def incoming_kernel(*refs):
    parts, weights_ref, out_hbm = refs[:6], refs[6], refs[8]
    wide_ref, kids_ref, out_ref, sems = refs[9:]
    cap = parts[0].shape[1]
    first = out_hbm.shape[2] - 6 * cap
    clear(wide_ref)
    copies = []
    for k in range(3):
        block = jnp.concatenate([parts[2 * k][...], parts[2 * k + 1][...]], axis=1).astype(F32)
        state = block[ROWS : ROWS + 1].astype(jnp.int32)

        def put(child, value, k=k):
            out_ref[k, child] = value

        bisect_tile(weights_ref[...], block[:ROWS], state, wide_ref, kids_ref, put)
        target = out_hbm.at[:, :, pl.ds(first + k * TILE, TILE)]
        copies.append(pltpu.make_async_copy(out_ref.at[k], target, sems.at[k]))
        copies[-1].start()
    for copy in copies:
        copy.wait()


def incoming_call(parts, weights, kept):
    return pl.pallas_call(
        incoming_kernel,
        in_specs=[VMEM_SPEC] * 7 + [HBM_SPEC],
        out_specs=HBM_SPEC,
        out_shape=jax.ShapeDtypeStruct(kept.shape, BF16),
        scratch_shapes=scratch_tiles()
        + [pltpu.VMEM((3, 2, ROWS, TILE), BF16), pltpu.SemaphoreType.DMA((3,))],
        input_output_aliases={7: 0},
        compiler_params=pltpu.CompilerParams(vmem_limit_bytes=LIMIT),
        name="incoming",
    )(*parts, weights, kept)


def shards(
    parents,
    refine,
    edge,
    move,
    face_owner,
    face_local,
    face_pair,
    face_orient,
    prolong,
    restrict,
    lift,
):
    count = parents.shape[2]
    slots = count + 6 * (count // 16)
    x = parents.reshape(ROWS, count)
    prolong = prolong.transpose(0, 2, 1, 3)
    owns = trace_call(x, face_owner, face_local, restrict.transpose(1, 0, 2))
    span2 = passed_along(owns[3], "gz", 1)
    span3 = passed_along(owns[2], "gz", -1)
    stream0 = passed_along(owns[1], "gx", 1)
    stream1 = passed_along(owns[0], "gx", -1)
    near = [stream0, stream1, span2, span3]
    own, meta, table, raised, place, code, state = plan_call(
        owns,
        face_owner,
        face_local,
        face_pair,
        face_orient,
        lift.transpose(2, 0, 1),
        move[None, :],
        refine[None, :],
        edge[None, :],
    )
    fixed, *packs = correct_call(x, own, near, meta, table, raised, place, code)
    parts = [passed_along(packs[k], ("gx", "gz"), OFFSETS[k]) for k in range(6)]
    kept, weights = home_call(fixed, state, prolong, slots)
    out = incoming_call(parts, weights, kept)
    return out.reshape(2, MODES, FIELDS, slots)


def solution(mesh):
    whole = ("gx", "gz")
    side = P(None, whole, None)
    in_specs = (P(None, None, whole), P(whole), P(whole), P(whole), side, side, side, side, P(), P(), P())
    out_specs = P(None, None, None, whole)
    return jax.shard_map(shards, mesh=mesh, in_specs=in_specs, out_specs=out_specs, check_vma=False)
```

```python
import functools

import jax
import jax.numpy as jnp
from jax import lax
from jax.experimental import pallas as pl
from jax.experimental.pallas import tpu as pltpu
from jax.sharding import PartitionSpec as P

MODES = 35
FMODES = 15
FIELDS = 8
ROWS = MODES * FIELDS
NODE_ROWS = FMODES * FIELDS
PAD = 40
LANES = 128
BUCKET = 512
WINDOW = 256
PART = 256
SETS = 4
LIMIT = 30 << 20
OFFSETS = (1, 2, 3, -1, -2, -3)
F32 = jnp.float32
BF16 = jnp.bfloat16
NT = (((1,), (1,)), ((), ()))


def passed_along(block, axis, distance):
    count = lax.axis_size(axis)
    return lax.ppermute(block, axis, [((i - distance) % count, i) for i in range(count)])


def face_table():
    nodes = [(a, b, 4 - a - b) for a in range(5) for b in range(5 - a)]
    index = {node: place for place, node in enumerate(nodes)}
    orders = [(0, 1, 2), (1, 2, 0), (2, 0, 1), (1, 0, 2), (0, 2, 1), (2, 1, 0)]
    return [[index[n[p[0]], n[p[1]], n[p[2]]] for n in nodes] for p in orders]


def iota(shape, dim):
    return lax.broadcasted_iota(jnp.int32, shape, dim)


def ones_where(mask):
    return jnp.where(mask, 1.0, 0.0).astype(BF16)


def match(rows, row):
    shape = (rows, row.shape[1])
    lines = lax.broadcasted_iota(jnp.int16, shape, 0)
    same = lines == jnp.broadcast_to(row.astype(jnp.int16), shape)
    return jnp.where(same, jnp.array(1, BF16), jnp.array(0, BF16))


def dot(a, b):
    return jnp.dot(a, b, preferred_element_type=F32)


def spread(small, rows, columns):
    height, width = small.shape
    left = ones_where(iota((rows, height), 0) // FIELDS == iota((rows, height), 1))
    right = ones_where(iota((width, columns), 0) == iota((width, columns), 1) // FIELDS)
    full = dot(dot(left, small).astype(BF16), right)
    same = iota((rows, columns), 0) % FIELDS == iota((rows, columns), 1) % FIELDS
    return jnp.where(same, full, 0.0)


VMEM_SPEC = pl.BlockSpec(memory_space=pltpu.VMEM)
SMEM_SPEC = pl.BlockSpec(memory_space=pltpu.SMEM)
HBM_SPEC = pl.BlockSpec(memory_space=pltpu.HBM)


def fetches(sources, targets, sems):
    copies = [pltpu.make_async_copy(a, b, sems.at[i]) for i, (a, b) in enumerate(zip(sources, targets))]
    for copy in copies:
        copy.start()
    return copies


def room(*arrays):
    buffers = [pltpu.VMEM(a.shape, a.dtype) for a in arrays]
    return buffers + [pltpu.SemaphoreType.DMA((len(arrays),))]


def trace_kernel(tile, *refs):
    sources, own_refs, every_ref, held, sems = refs[:4], refs[4:8], refs[8], refs[9:13], refs[13]
    restrict_ref, owner_ref, local_ref, x_ref = held
    copies = fetches(sources, held, sems)
    count = x_ref.shape[1]
    faces = owner_ref.shape[2]
    copies[0].wait()
    spreads = [spread(restrict_ref[:, l, :], NODE_ROWS, ROWS) for l in range(4)]
    every_ref[...] = jnp.concatenate(spreads, axis=0).astype(BF16)
    for copy in copies[1:]:
        copy.wait()
    for s in range(4):

        def step(j, carry, s=s):
            lanes = pl.ds(pl.multiple_of(j * tile, tile), tile)
            owner = owner_ref[s, :, lanes]
            local = local_ref[s, :, lanes]
            onehot = match(count, owner)
            picked = dot(x_ref[...], onehot).astype(BF16)
            traces = dot(every_ref[...], picked)
            chosen = traces[:NODE_ROWS]
            for l in range(1, 4):
                chosen = jnp.where(local == l, traces[l * NODE_ROWS : (l + 1) * NODE_ROWS], chosen)
            own_refs[s][:, lanes] = chosen.astype(BF16)
            return carry

        lax.fori_loop(0, faces // tile, step, 0)


def trace_call(x, owner, local, restrict):
    faces = owner.shape[2]
    return pl.pallas_call(
        functools.partial(trace_kernel, 1024),
        in_specs=[HBM_SPEC] * 4,
        out_specs=[VMEM_SPEC] * 4,
        out_shape=[jax.ShapeDtypeStruct((NODE_ROWS, faces), BF16)] * 4,
        scratch_shapes=[pltpu.VMEM((4 * NODE_ROWS, ROWS), BF16)] + room(restrict, owner, local, x),
        compiler_params=pltpu.CompilerParams(vmem_limit_bytes=LIMIT),
        cost_estimate=pl.CostEstimate(flops=10**10, bytes_accessed=10**7, transcendentals=0),
        name="trace",
    )(*[pltpu.with_memory_space_constraint(a, pltpu.HBM) for a in (restrict, owner, local, x)])


def rank_moves(move_ref, refine_ref, edge_ref, place_ref, code_ref, state_ref):
    count = move_ref.shape[1]
    block = 256
    cap = count // 16
    before = ones_where(iota((block, block), 0) < iota((block, block), 1))
    seen = jnp.zeros((8, 1), F32)
    which = iota((8, block), 0)
    for b in range(count // block):
        at = slice(b * block, (b + 1) * block)
        move = move_ref[:, at]
        hit = jnp.where(which == move, 1.0, 0.0)
        earlier = dot(hit.astype(BF16), before) + seen
        rank = jnp.sum(hit * earlier, axis=0, keepdims=True).astype(jnp.int32)
        place_ref[:, at] = jnp.where(move < 6, move * cap + rank, 6 * cap)
        seen = seen + jnp.sum(hit, axis=1, keepdims=True)
        code = jnp.where(refine_ref[:, at] == 1, edge_ref[:, at] + 1, 0)
        code_ref[:, at] = code
        state_ref[:, at] = jnp.where(move == 6, code, -1)


def plan_kernel(*refs):
    own_refs, sources, held, sems = refs[:4], refs[4:12], refs[19:27], refs[27]
    own_ref, meta_ref, table_ref, raised_ref, place_ref, code_ref, state_ref = refs[12:19]
    owner_ref, local_ref, pair_ref, orient_ref, lift_ref, move_ref, refine_ref, edge_ref = held
    for copy in fetches(sources, held, sems):
        copy.wait()
    rank_moves(move_ref, refine_ref, edge_ref, place_ref, code_ref, state_ref)
    raised = [spread(lift_ref[:, l, :].astype(BF16), NODE_ROWS, ROWS) for l in range(4)]
    raised_ref[...] = jnp.concatenate(raised, axis=0).T.astype(BF16)
    faces = owner_ref.shape[2]
    block = 256
    before = ones_where(iota((block, block), 0) < iota((block, block), 1))
    eight = iota((8, faces), 0)
    buckets = [owner_ref[s] // BUCKET for s in range(4)]
    hits = jnp.concatenate([jnp.where(eight == b, 1.0, 0.0) for b in buckets], axis=0)
    smaller = jnp.concatenate([jnp.where(b < eight, 1.0, 0.0) for b in buckets], axis=0)
    start = jnp.sum(smaller, axis=1, keepdims=True)
    end = start + jnp.sum(hits, axis=1, keepdims=True)
    first = start.astype(jnp.int32)
    last = end.astype(jnp.int32)
    begin = jnp.minimum(first // LANES * LANES, faces - LANES)
    trips = (last - begin + WINDOW - 1) // WINDOW
    longest = jnp.maximum(
        jnp.maximum(trips[0:8], trips[8:16]), jnp.maximum(trips[16:24], trips[24:32])
    )
    longest = jnp.concatenate([longest] * 4, axis=0)
    lane = iota((32, LANES), 1)
    table_ref[...] = jnp.where(lane == 0, begin, jnp.where(lane == 1, trips, longest))
    seen = start
    places = []
    for b in range(faces // block):
        part = hits[:, b * block : (b + 1) * block]
        places.append(part * (dot(part.astype(BF16), before) + seen))
        seen = seen + jnp.sum(part, axis=1, keepdims=True)
    places = jnp.concatenate(places, axis=1)
    meta_ref[...] = jnp.full(meta_ref.shape, -1, jnp.int32)
    for s in range(4):
        spot = jnp.sum(places[8 * s : 8 * s + 8], axis=0, keepdims=True).astype(jnp.int32)
        order = match(faces, spot)
        owner, pair = owner_ref[s], pair_ref[s]
        values = (owner // 256, owner % 256, local_ref[s], pair // 256, pair % 256, orient_ref[s])
        small = jnp.zeros((8, faces), jnp.int32)
        for row, value in enumerate(values):
            small = jnp.where(eight == row, value, small)
        both = jnp.concatenate([own_refs[s][...].astype(F32), small.astype(F32)], axis=0)
        moved = lax.dot_general(both.astype(BF16), order, NT, preferred_element_type=F32)
        own_ref[s] = moved[:NODE_ROWS].astype(BF16)
        got = moved[NODE_ROWS:].astype(jnp.int32)
        rows = (got[0:1] * 256 + got[1:2], got[2:3], got[3:4] * 256 + got[4:5], got[5:6])
        meta = jnp.zeros((8, faces), jnp.int32)
        for row, value in enumerate(rows):
            meta = jnp.where(eight == row, value, meta)
        meta_ref[s, :, :faces] = meta


def plan_call(owns, *rest):
    faces = rest[0].shape[2]
    flat = jax.ShapeDtypeStruct(rest[-1].shape, jnp.int32)
    return pl.pallas_call(
        plan_kernel,
        in_specs=[VMEM_SPEC] * 4 + [HBM_SPEC] * 8,
        out_specs=[VMEM_SPEC] * 7,
        out_shape=[
            jax.ShapeDtypeStruct((4, NODE_ROWS, faces), BF16),
            jax.ShapeDtypeStruct((4, 8, faces + LANES), jnp.int32),
            jax.ShapeDtypeStruct((32, LANES), jnp.int32),
            jax.ShapeDtypeStruct((ROWS, 4 * NODE_ROWS), BF16),
            flat,
            flat,
            flat,
        ],
        scratch_shapes=room(*rest),
        compiler_params=pltpu.CompilerParams(vmem_limit_bytes=LIMIT),
        cost_estimate=pl.CostEstimate(flops=5 * 10**9, bytes_accessed=4 * 10**6, transcendentals=0),
        name="plan",
    )(*owns, *rest)


def correct_kernel(tile, *refs):
    raised_ref, x_hbm, own_ref = refs[:3]
    near_refs = refs[3:7]
    meta_ref, table_ref, place_ref, code_ref, fixed_ref = refs[7:12]
    pack_refs = refs[12:18]
    lifted_ref, payload_ref, total_ref, x_ref, sems = refs[18:]
    copies = fetches((x_hbm,), (x_ref,), sems)
    count = x_ref.shape[1]
    faces = own_ref.shape[2]
    cap = pack_refs[0].shape[1]
    table = face_table()

    def jumps(j, carry):
        lanes = pl.ds(pl.multiple_of(j * tile, tile), tile)
        for s in range(4):
            local = meta_ref[s, 1:2, lanes]
            pair = meta_ref[s, 2:3, lanes]
            orient = meta_ref[s, 3:4, lanes]
            matcher = match(faces, pair)
            paired = dot(near_refs[s][...], matcher)
            own = own_ref[s, :, lanes].astype(F32)
            jump = []
            for n in range(FMODES):
                best = paired[table[0][n] * FIELDS : (table[0][n] + 1) * FIELDS]
                for o in range(1, 6):
                    if table[o][n] != table[0][n]:
                        other = paired[table[o][n] * FIELDS : (table[o][n] + 1) * FIELDS]
                        best = jnp.where(orient == o, other, best)
                jump.append(0.5 * (best - own[n * FIELDS : (n + 1) * FIELDS]))
            jump = jnp.concatenate(jump, axis=0)
            split = jnp.concatenate([jnp.where(local == l, jump, 0.0) for l in range(4)], axis=0)
            lifted_ref[s, :, lanes] = dot(raised_ref[...], split.astype(BF16)).astype(BF16)
        return carry

    for s in range(4):
        lifted_ref[s, :, faces:] = jnp.zeros((ROWS, LANES), BF16)
    lax.fori_loop(0, faces // tile, jumps, 0)
    copies[0].wait()

    def fix(t, carry):
        at = pl.ds(pl.multiple_of(t * BUCKET, BUCKET), BUCKET)

        def window(s, i):
            begin = table_ref[8 * s + t, 0] + i * WINDOW
            lanes = pl.ds(pl.multiple_of(begin, LANES), WINDOW)
            return lifted_ref[s, :, lanes], match(BUCKET, meta_ref[s, 0:1, lanes] - t * BUCKET)

        both = [window(s, 0) for s in range(4)]
        total = x_ref[:, at].astype(F32) + lax.dot_general(
            jnp.concatenate([a for a, _ in both], axis=1),
            jnp.concatenate([b for _, b in both], axis=1),
            NT,
            preferred_element_type=F32,
        )
        total_ref[...] = total

        @pl.when(table_ref[t, 2] > 1)
        def _():
            for s in range(4):

                def more(i, carry, s=s):
                    a, b = window(s, i)
                    total_ref[...] += lax.dot_general(a, b, NT, preferred_element_type=F32)
                    return carry

                lax.fori_loop(1, table_ref[8 * s + t, 1], more, 0)

        total = total_ref[...]
        fixed_ref[:, at] = total.astype(BF16)
        code = jnp.broadcast_to(code_ref[:, at], (8, BUCKET)).astype(F32)
        payload_ref[:, at] = jnp.concatenate([total, code], axis=0).astype(BF16)
        return carry

    lax.fori_loop(0, count // BUCKET, fix, 0)
    for k, pack_ref in enumerate(pack_refs):
        packer = match(cap, place_ref[...] - k * cap)
        pack_ref[...] = lax.dot_general(
            payload_ref[...], packer, NT, preferred_element_type=F32
        ).astype(BF16)


def correct_call(x, own, near, meta, table, raised, place, code):
    count = x.shape[1]
    cap = count // 16
    faces = own.shape[2]
    rows = ROWS + 8
    return pl.pallas_call(
        functools.partial(correct_kernel, 512),
        in_specs=[VMEM_SPEC, HBM_SPEC] + [VMEM_SPEC] * 6 + [SMEM_SPEC] + [VMEM_SPEC] * 2,
        out_specs=[VMEM_SPEC] * 7,
        out_shape=[jax.ShapeDtypeStruct((ROWS, count), BF16)]
        + [jax.ShapeDtypeStruct((rows, cap), BF16)] * 6,
        scratch_shapes=[
            pltpu.VMEM((4, ROWS, faces + LANES), BF16),
            pltpu.VMEM((rows, count), BF16),
            pltpu.VMEM((ROWS, BUCKET), F32),
        ]
        + room(x),
        compiler_params=pltpu.CompilerParams(vmem_limit_bytes=LIMIT),
        cost_estimate=pl.CostEstimate(flops=10**10, bytes_accessed=10**7, transcendentals=0),
        name="correct",
    )(raised, x, own, *near, meta, table, place, code)


def joined_weights(prolong_ref):
    rows = []
    for c in range(2):
        total = jnp.zeros((PAD, 6 * PAD), F32)
        for e in range(6):
            left = ones_where(iota((PAD, MODES), 0) == iota((PAD, MODES), 1))
            right = ones_where(iota((MODES, 6 * PAD), 0) + e * PAD == iota((MODES, 6 * PAD), 1))
            total += dot(dot(left, prolong_ref[e, :, c, :]).astype(BF16), right)
        rows.append(total)
    return jnp.concatenate(rows, axis=0).astype(BF16)


def bisect_part(weights, parents, state, wide_ref, kids_ref, put):
    pieces = [slice(i * LANES, (i + 1) * LANES) for i in range(PART // LANES)]
    parents = jnp.where(state >= 0, parents, 0.0)
    shape = (2 * PAD, PART)
    second = (iota(shape, 0) // PAD).astype(jnp.int16)
    cut = jnp.broadcast_to((state - 1).astype(jnp.int16), shape) - second
    for i, piece in enumerate(pieces):
        wide_ref[i, :ROWS, :] = parents[:, piece]
    for f in range(FIELDS):
        modes = [wide_ref[i, pl.ds(f, PAD, stride=FIELDS), :] for i in range(len(pieces))]
        modes = jnp.concatenate(modes, axis=1)
        twice = jnp.concatenate([modes, modes], axis=0).astype(BF16)
        masked = [jnp.where(cut == 2 * i, twice, jnp.array(0, BF16)) for i in range(3)]
        both = dot(weights, jnp.concatenate(masked, axis=0))
        for i, piece in enumerate(pieces):
            kids_ref[i, pl.ds(f, MODES, stride=FIELDS), :] = both[:MODES, piece]
            kids_ref[i, pl.ds(ROWS + f, MODES, stride=FIELDS), :] = both[PAD : PAD + MODES, piece]
    kids = jnp.concatenate([kids_ref[i] for i in range(len(pieces))], axis=1)
    put(0, jnp.where(state == 0, parents, kids[:ROWS]).astype(BF16))
    put(1, kids[ROWS:].astype(BF16))


def scratch_sets():
    wide = pltpu.VMEM((PART // LANES, PAD * FIELDS, LANES), F32)
    kids = pltpu.VMEM((PART // LANES, 2 * ROWS, LANES), F32)
    return [wide] * SETS + [kids] * SETS


def clear(wide_refs):
    for wide_ref in wide_refs:
        wide_ref[:, ROWS:, :] = jnp.zeros((PART // LANES, PAD * FIELDS - ROWS, LANES), F32)


def home_kernel(fixed_ref, state_ref, prolong_ref, out_ref, weights_ref, *scratch):
    wide_refs, kids_refs = scratch[:SETS], scratch[SETS:]
    t = pl.program_id(0)

    @pl.when(t == 0)
    def _():
        weights_ref[...] = joined_weights(prolong_ref)
        clear(wide_refs)

    for h in range(SETS):
        at = pl.ds(pl.multiple_of(t * (SETS * PART) + h * PART, PART), PART)

        def put(child, value, h=h):
            out_ref[child, :, h * PART : (h + 1) * PART] = value

        parents = fixed_ref[:, at].astype(F32)
        bisect_part(weights_ref[...], parents, state_ref[:, at], wide_refs[h], kids_refs[h], put)


def home_call(fixed, state, prolong, slots):
    count = fixed.shape[1]
    tile = SETS * PART
    return pl.pallas_call(
        home_kernel,
        grid=(count // tile,),
        in_specs=[VMEM_SPEC, VMEM_SPEC, VMEM_SPEC],
        out_specs=[
            pl.BlockSpec((2, ROWS, tile), lambda i: (0, 0, i)),
            pl.BlockSpec((2 * PAD, 6 * PAD), lambda i: (0, 0)),
        ],
        out_shape=[
            jax.ShapeDtypeStruct((2, ROWS, slots), BF16),
            jax.ShapeDtypeStruct((2 * PAD, 6 * PAD), BF16),
        ],
        scratch_shapes=scratch_sets(),
        compiler_params=pltpu.CompilerParams(vmem_limit_bytes=LIMIT),
        cost_estimate=pl.CostEstimate(
            flops=2 * 560 * 280 * count, bytes_accessed=6 * ROWS * count, transcendentals=0
        ),
        name="home",
    )(fixed, state, prolong)


def incoming_kernel(*refs):
    parts, weights_ref, out_hbm = refs[:6], refs[6], refs[8]
    wide_refs, kids_refs = refs[9 : 9 + SETS], refs[9 + SETS : 9 + 2 * SETS]
    out_ref, sems = refs[9 + 2 * SETS :]
    cap = parts[0].shape[1]
    first = out_hbm.shape[2] - 6 * cap
    clear(wide_refs)
    copies = []
    for k in range(6):
        block = parts[k][...].astype(F32)
        state = block[ROWS : ROWS + 1].astype(jnp.int32)

        def put(child, value, k=k):
            out_ref[k, child] = value

        h = k % SETS
        bisect_part(weights_ref[...], block[:ROWS], state, wide_refs[h], kids_refs[h], put)
        target = out_hbm.at[:, :, pl.ds(first + k * cap, cap)]
        copies.append(pltpu.make_async_copy(out_ref.at[k], target, sems.at[k]))
        copies[-1].start()
    for copy in copies:
        copy.wait()


def incoming_call(parts, weights, kept):
    return pl.pallas_call(
        incoming_kernel,
        in_specs=[VMEM_SPEC] * 7 + [HBM_SPEC],
        out_specs=HBM_SPEC,
        out_shape=jax.ShapeDtypeStruct(kept.shape, BF16),
        scratch_shapes=scratch_sets()
        + [pltpu.VMEM((6, 2, ROWS, PART), BF16), pltpu.SemaphoreType.DMA((6,))],
        input_output_aliases={7: 0},
        compiler_params=pltpu.CompilerParams(vmem_limit_bytes=LIMIT),
        name="incoming",
    )(*parts, weights, kept)


def shards(
    parents,
    refine,
    edge,
    move,
    face_owner,
    face_local,
    face_pair,
    face_orient,
    prolong,
    restrict,
    lift,
):
    count = parents.shape[2]
    slots = count + 6 * (count // 16)
    x = parents.reshape(ROWS, count)
    prolong = prolong.transpose(0, 2, 1, 3)
    owns = trace_call(x, face_owner, face_local, restrict.transpose(1, 0, 2))
    span2 = passed_along(owns[3], "gz", 1)
    span3 = passed_along(owns[2], "gz", -1)
    stream0 = passed_along(owns[1], "gx", 1)
    stream1 = passed_along(owns[0], "gx", -1)
    near = [stream0, stream1, span2, span3]
    own, meta, table, raised, place, code, state = plan_call(
        owns,
        face_owner,
        face_local,
        face_pair,
        face_orient,
        lift.transpose(2, 0, 1),
        move[None, :],
        refine[None, :],
        edge[None, :],
    )
    fixed, *packs = correct_call(x, own, near, meta, table, raised, place, code)
    parts = [passed_along(packs[k], ("gx", "gz"), OFFSETS[k]) for k in range(6)]
    kept, weights = home_call(fixed, state, prolong, slots)
    out = incoming_call(parts, weights, kept)
    return out.reshape(2, MODES, FIELDS, slots)


def solution(mesh):
    whole = ("gx", "gz")
    side = P(None, whole, None)
    in_specs = (P(None, None, whole), P(whole), P(whole), P(whole), side, side, side, side, P(), P(), P())
    out_specs = P(None, None, None, whole)
    return jax.shard_map(shards, mesh=mesh, in_specs=in_specs, out_specs=out_specs, check_vma=False)
```

```python
import functools

import jax
import jax.numpy as jnp
from jax import lax
from jax.experimental import pallas as pl
from jax.experimental.pallas import tpu as pltpu
from jax.sharding import PartitionSpec as P

MODES = 35
FMODES = 15
FIELDS = 8
ROWS = MODES * FIELDS
NODE_ROWS = FMODES * FIELDS
PAD = 40
LANES = 128
BUCKET = 512
WINDOW = 256
PART = 256
SETS = 4
LIMIT = 30 << 20
OFFSETS = (1, 2, 3, -1, -2, -3)
FORWARD = (1, 2, 0)
BACKWARD = (4, 5, 3)
F32 = jnp.float32
BF16 = jnp.bfloat16
NT = (((1,), (1,)), ((), ()))


def passed_along(block, axis, distance):
    count = lax.axis_size(axis)
    return lax.ppermute(block, axis, [((i - distance) % count, i) for i in range(count)])


def face_table():
    nodes = [(a, b, 4 - a - b) for a in range(5) for b in range(5 - a)]
    index = {node: place for place, node in enumerate(nodes)}
    orders = [(0, 1, 2), (1, 2, 0), (2, 0, 1), (1, 0, 2), (0, 2, 1), (2, 1, 0)]
    return [[index[n[p[0]], n[p[1]], n[p[2]]] for n in nodes] for p in orders]


def iota(shape, dim):
    return lax.broadcasted_iota(jnp.int32, shape, dim)


def ones_where(mask):
    return jnp.where(mask, 1.0, 0.0).astype(BF16)


def match(rows, row):
    shape = (rows, row.shape[1])
    lines = lax.broadcasted_iota(jnp.int16, shape, 0)
    same = lines == jnp.broadcast_to(row.astype(jnp.int16), shape)
    return jnp.where(same, jnp.array(1, BF16), jnp.array(0, BF16))


def dot(a, b):
    return jnp.dot(a, b, preferred_element_type=F32)


def spread(small, rows, columns):
    height, width = small.shape
    left = ones_where(iota((rows, height), 0) // FIELDS == iota((rows, height), 1))
    right = ones_where(iota((width, columns), 0) == iota((width, columns), 1) // FIELDS)
    full = dot(dot(left, small).astype(BF16), right)
    same = iota((rows, columns), 0) % FIELDS == iota((rows, columns), 1) % FIELDS
    return jnp.where(same, full, 0.0)


VMEM_SPEC = pl.BlockSpec(memory_space=pltpu.VMEM)
SMEM_SPEC = pl.BlockSpec(memory_space=pltpu.SMEM)
HBM_SPEC = pl.BlockSpec(memory_space=pltpu.HBM)


def fetches(sources, targets, sems):
    copies = [pltpu.make_async_copy(a, b, sems.at[i]) for i, (a, b) in enumerate(zip(sources, targets))]
    for copy in copies:
        copy.start()
    return copies


def room(*arrays):
    buffers = [pltpu.VMEM(a.shape, a.dtype) for a in arrays]
    return buffers + [pltpu.SemaphoreType.DMA((len(arrays),))]


def trace_kernel(tile, *refs):
    sources, own_refs, every_ref, held, sems = refs[:4], refs[4:8], refs[8], refs[9:13], refs[13]
    restrict_ref, owner_ref, local_ref, x_ref = held
    copies = fetches(sources, held, sems)
    count = x_ref.shape[1]
    faces = owner_ref.shape[2]
    copies[0].wait()
    spreads = [spread(restrict_ref[:, l, :], NODE_ROWS, ROWS) for l in range(4)]
    every_ref[...] = jnp.concatenate(spreads, axis=0).astype(BF16)
    for copy in copies[1:]:
        copy.wait()
    for s in range(4):

        def step(j, carry, s=s):
            lanes = pl.ds(pl.multiple_of(j * tile, tile), tile)
            owner = owner_ref[s, :, lanes]
            local = local_ref[s, :, lanes]
            onehot = match(count, owner)
            picked = dot(x_ref[...], onehot).astype(BF16)
            traces = dot(every_ref[...], picked)
            chosen = traces[:NODE_ROWS]
            for l in range(1, 4):
                chosen = jnp.where(local == l, traces[l * NODE_ROWS : (l + 1) * NODE_ROWS], chosen)
            own_refs[s][:, lanes] = chosen.astype(BF16)
            return carry

        lax.fori_loop(0, faces // tile, step, 0)


def trace_call(x, owner, local, restrict):
    faces = owner.shape[2]
    return pl.pallas_call(
        functools.partial(trace_kernel, 1024),
        in_specs=[HBM_SPEC] * 4,
        out_specs=[VMEM_SPEC] * 4,
        out_shape=[jax.ShapeDtypeStruct((NODE_ROWS, faces), BF16)] * 4,
        scratch_shapes=[pltpu.VMEM((4 * NODE_ROWS, ROWS), BF16)] + room(restrict, owner, local, x),
        compiler_params=pltpu.CompilerParams(vmem_limit_bytes=LIMIT),
        cost_estimate=pl.CostEstimate(flops=10**10, bytes_accessed=10**7, transcendentals=0),
        name="trace",
    )(*[pltpu.with_memory_space_constraint(a, pltpu.HBM) for a in (restrict, owner, local, x)])


def rank_moves(move_ref, refine_ref, edge_ref, place_ref, code_ref, state_ref):
    count = move_ref.shape[1]
    block = 256
    cap = count // 16
    before = ones_where(iota((block, block), 0) < iota((block, block), 1))
    seen = jnp.zeros((8, 1), F32)
    which = iota((8, block), 0)
    for b in range(count // block):
        at = slice(b * block, (b + 1) * block)
        move = move_ref[:, at]
        hit = jnp.where(which == move, 1.0, 0.0)
        earlier = dot(hit.astype(BF16), before) + seen
        rank = jnp.sum(hit * earlier, axis=0, keepdims=True).astype(jnp.int32)
        place_ref[:, at] = jnp.where(move < 6, move * cap + rank, 6 * cap)
        seen = seen + jnp.sum(hit, axis=1, keepdims=True)
        code = jnp.where(refine_ref[:, at] == 1, edge_ref[:, at] + 1, 0)
        code_ref[:, at] = code
        state_ref[:, at] = jnp.where(move == 6, code, -1)


def plan_kernel(*refs):
    own_refs, sources, held, sems = refs[:4], refs[4:12], refs[19:27], refs[27]
    own_ref, meta_ref, table_ref, raised_ref, place_ref, code_ref, state_ref = refs[12:19]
    owner_ref, local_ref, pair_ref, orient_ref, lift_ref, move_ref, refine_ref, edge_ref = held
    for copy in fetches(sources, held, sems):
        copy.wait()
    rank_moves(move_ref, refine_ref, edge_ref, place_ref, code_ref, state_ref)
    raised = [spread(lift_ref[:, l, :].astype(BF16), NODE_ROWS, ROWS) for l in range(4)]
    raised_ref[...] = jnp.concatenate(raised, axis=0).T.astype(BF16)
    faces = owner_ref.shape[2]
    block = 256
    before = ones_where(iota((block, block), 0) < iota((block, block), 1))
    eight = iota((8, faces), 0)
    buckets = [owner_ref[s] // BUCKET for s in range(4)]
    hits = jnp.concatenate([jnp.where(eight == b, 1.0, 0.0) for b in buckets], axis=0)
    smaller = jnp.concatenate([jnp.where(b < eight, 1.0, 0.0) for b in buckets], axis=0)
    start = jnp.sum(smaller, axis=1, keepdims=True)
    end = start + jnp.sum(hits, axis=1, keepdims=True)
    first = start.astype(jnp.int32)
    last = end.astype(jnp.int32)
    begin = jnp.minimum(first // LANES * LANES, faces - LANES)
    trips = (last - begin + WINDOW - 1) // WINDOW
    longest = jnp.maximum(
        jnp.maximum(trips[0:8], trips[8:16]), jnp.maximum(trips[16:24], trips[24:32])
    )
    longest = jnp.concatenate([longest] * 4, axis=0)
    lane = iota((32, LANES), 1)
    table_ref[...] = jnp.where(lane == 0, begin, jnp.where(lane == 1, trips, longest))
    seen = start
    places = []
    for b in range(faces // block):
        part = hits[:, b * block : (b + 1) * block]
        places.append(part * (dot(part.astype(BF16), before) + seen))
        seen = seen + jnp.sum(part, axis=1, keepdims=True)
    places = jnp.concatenate(places, axis=1)
    meta_ref[...] = jnp.full(meta_ref.shape, -1, jnp.int32)
    for s in range(4):
        spot = jnp.sum(places[8 * s : 8 * s + 8], axis=0, keepdims=True).astype(jnp.int32)
        order = match(faces, spot)
        owner, pair = owner_ref[s], pair_ref[s]
        values = (owner // 256, owner % 256, local_ref[s], pair // 256, pair % 256, orient_ref[s])
        small = jnp.zeros((8, faces), jnp.int32)
        for row, value in enumerate(values):
            small = jnp.where(eight == row, value, small)
        both = jnp.concatenate([own_refs[s][...].astype(F32), small.astype(F32)], axis=0)
        moved = lax.dot_general(both.astype(BF16), order, NT, preferred_element_type=F32)
        own_ref[s] = moved[:NODE_ROWS].astype(BF16)
        got = moved[NODE_ROWS:].astype(jnp.int32)
        rows = (got[0:1] * 256 + got[1:2], got[2:3], got[3:4] * 256 + got[4:5], got[5:6])
        meta = jnp.zeros((8, faces), jnp.int32)
        for row, value in enumerate(rows):
            meta = jnp.where(eight == row, value, meta)
        meta_ref[s, :, :faces] = meta


def plan_call(owns, *rest):
    faces = rest[0].shape[2]
    flat = jax.ShapeDtypeStruct(rest[-1].shape, jnp.int32)
    return pl.pallas_call(
        plan_kernel,
        in_specs=[VMEM_SPEC] * 4 + [HBM_SPEC] * 8,
        out_specs=[VMEM_SPEC] * 7,
        out_shape=[
            jax.ShapeDtypeStruct((4, NODE_ROWS, faces), BF16),
            jax.ShapeDtypeStruct((4, 8, faces + LANES), jnp.int32),
            jax.ShapeDtypeStruct((32, LANES), jnp.int32),
            jax.ShapeDtypeStruct((ROWS, 4 * NODE_ROWS), BF16),
            flat,
            flat,
            flat,
        ],
        scratch_shapes=room(*rest),
        compiler_params=pltpu.CompilerParams(vmem_limit_bytes=LIMIT),
        cost_estimate=pl.CostEstimate(flops=5 * 10**9, bytes_accessed=4 * 10**6, transcendentals=0),
        name="plan",
    )(*owns, *rest)


def correct_kernel(tile, moves, *refs):
    raised_ref, x_hbm, own_ref = refs[:3]
    near_refs = refs[3:7]
    meta_ref, table_ref, place_ref, code_ref, payload_ref = refs[7:12]
    pack_refs = refs[12 : 12 + len(moves)]
    lifted_ref, total_ref, x_ref, sems = refs[12 + len(moves) :]
    copies = fetches((x_hbm,), (x_ref,), sems)
    count = x_ref.shape[1]
    faces = own_ref.shape[2]
    table = face_table()

    def jumps(j, carry):
        lanes = pl.ds(pl.multiple_of(j * tile, tile), tile)
        for s in range(4):
            local = meta_ref[s, 1:2, lanes]
            pair = meta_ref[s, 2:3, lanes]
            orient = meta_ref[s, 3:4, lanes]
            matcher = match(faces, pair)
            paired = dot(near_refs[s][...], matcher)
            own = own_ref[s, :, lanes].astype(F32)
            jump = []
            for n in range(FMODES):
                best = paired[table[0][n] * FIELDS : (table[0][n] + 1) * FIELDS]
                for o in range(1, 6):
                    if table[o][n] != table[0][n]:
                        other = paired[table[o][n] * FIELDS : (table[o][n] + 1) * FIELDS]
                        best = jnp.where(orient == o, other, best)
                jump.append(0.5 * (best - own[n * FIELDS : (n + 1) * FIELDS]))
            jump = jnp.concatenate(jump, axis=0)
            split = jnp.concatenate([jnp.where(local == l, jump, 0.0) for l in range(4)], axis=0)
            lifted_ref[s, :, lanes] = dot(raised_ref[...], split.astype(BF16)).astype(BF16)
        return carry

    for s in range(4):
        lifted_ref[s, :, faces:] = jnp.zeros((ROWS, LANES), BF16)
    lax.fori_loop(0, faces // tile, jumps, 0)
    copies[0].wait()

    def window(s, t, i):
        begin = table_ref[8 * s + t, 0] + i * WINDOW
        lanes = pl.ds(pl.multiple_of(begin, LANES), WINDOW)
        return lifted_ref[s, :, lanes], match(BUCKET, meta_ref[s, 0:1, lanes] - t * BUCKET)

    def fix(pair, carry):
        buckets = [2 * pair, 2 * pair + 1]
        spots = [pl.ds(pl.multiple_of(t * BUCKET, BUCKET), BUCKET) for t in buckets]
        for u, (t, at) in enumerate(zip(buckets, spots)):
            both = [window(s, t, 0) for s in range(4)]
            total_ref[u] = x_ref[:, at].astype(F32) + lax.dot_general(
                jnp.concatenate([a for a, _ in both], axis=1),
                jnp.concatenate([b for _, b in both], axis=1),
                NT,
                preferred_element_type=F32,
            )

        @pl.when(jnp.maximum(table_ref[buckets[0], 2], table_ref[buckets[1], 2]) > 1)
        def _():
            for u, t in enumerate(buckets):
                for s in range(4):

                    def more(i, carry, s=s, t=t, u=u):
                        a, b = window(s, t, i)
                        total_ref[u] += lax.dot_general(a, b, NT, preferred_element_type=F32)
                        return carry

                    lax.fori_loop(1, table_ref[8 * s + t, 1], more, 0)

        for u, at in enumerate(spots):
            code = jnp.broadcast_to(code_ref[:, at], (8, BUCKET)).astype(F32)
            payload_ref[:, at] = jnp.concatenate([total_ref[u], code], axis=0).astype(BF16)
        return carry

    lax.fori_loop(0, count // (2 * BUCKET), fix, 0)
    pack_moves(moves, payload_ref, place_ref, pack_refs)


def pack_moves(moves, payload_ref, place_ref, pack_refs):
    for k, pack_ref in zip(moves, pack_refs):
        cap = pack_ref.shape[1]
        packer = match(cap, place_ref[...] - k * cap)
        pack_ref[...] = lax.dot_general(
            payload_ref[...], packer, NT, preferred_element_type=F32
        ).astype(BF16)


def pack_kernel(moves, payload_ref, place_ref, *pack_refs):
    pack_moves(moves, payload_ref, place_ref, pack_refs)


def pack_call(moves, payload, place):
    rows, count = payload.shape
    return pl.pallas_call(
        functools.partial(pack_kernel, moves),
        in_specs=[VMEM_SPEC] * 2,
        out_specs=[VMEM_SPEC] * len(moves),
        out_shape=[jax.ShapeDtypeStruct((rows, count // 16), BF16)] * len(moves),
        compiler_params=pltpu.CompilerParams(vmem_limit_bytes=LIMIT),
        cost_estimate=pl.CostEstimate(flops=2 * 10**9, bytes_accessed=10**6, transcendentals=0),
        name="pack",
    )(payload, place)


def correct_call(moves, x, own, near, meta, table, raised, place, code):
    count = x.shape[1]
    cap = count // 16
    faces = own.shape[2]
    rows = ROWS + 8
    return pl.pallas_call(
        functools.partial(correct_kernel, 512, moves),
        in_specs=[VMEM_SPEC, HBM_SPEC] + [VMEM_SPEC] * 6 + [SMEM_SPEC] + [VMEM_SPEC] * 2,
        out_specs=[VMEM_SPEC] * (1 + len(moves)),
        out_shape=[jax.ShapeDtypeStruct((rows, count), BF16)]
        + [jax.ShapeDtypeStruct((rows, cap), BF16)] * len(moves),
        scratch_shapes=[
            pltpu.VMEM((4, ROWS, faces + LANES), BF16),
            pltpu.VMEM((2, ROWS, BUCKET), F32),
        ]
        + room(x),
        compiler_params=pltpu.CompilerParams(vmem_limit_bytes=LIMIT),
        cost_estimate=pl.CostEstimate(flops=10**10, bytes_accessed=10**7, transcendentals=0),
        name="correct",
    )(raised, x, own, *near, meta, table, place, code)


def joined_weights(prolong_ref):
    rows = []
    for c in range(2):
        total = jnp.zeros((PAD, 6 * PAD), F32)
        for e in range(6):
            left = ones_where(iota((PAD, MODES), 0) == iota((PAD, MODES), 1))
            right = ones_where(iota((MODES, 6 * PAD), 0) + e * PAD == iota((MODES, 6 * PAD), 1))
            total += dot(dot(left, prolong_ref[e, :, c, :]).astype(BF16), right)
        rows.append(total)
    return jnp.concatenate(rows, axis=0).astype(BF16)


def bisect_part(weights, parents, state, wide_ref, kids_ref, put):
    pieces = [slice(i * LANES, (i + 1) * LANES) for i in range(PART // LANES)]
    parents = jnp.where(state >= 0, parents, 0.0)
    shape = (2 * PAD, PART)
    second = (iota(shape, 0) // PAD).astype(jnp.int16)
    cut = jnp.broadcast_to((state - 1).astype(jnp.int16), shape) - second
    for i, piece in enumerate(pieces):
        wide_ref[i, :ROWS, :] = parents[:, piece]
    for f in range(FIELDS):
        modes = [wide_ref[i, pl.ds(f, PAD, stride=FIELDS), :] for i in range(len(pieces))]
        modes = jnp.concatenate(modes, axis=1)
        twice = jnp.concatenate([modes, modes], axis=0).astype(BF16)
        masked = [jnp.where(cut == 2 * i, twice, jnp.array(0, BF16)) for i in range(3)]
        both = dot(weights, jnp.concatenate(masked, axis=0))
        for i, piece in enumerate(pieces):
            kids_ref[i, pl.ds(f, MODES, stride=FIELDS), :] = both[:MODES, piece]
            kids_ref[i, pl.ds(ROWS + f, MODES, stride=FIELDS), :] = both[PAD : PAD + MODES, piece]
    kids = jnp.concatenate([kids_ref[i] for i in range(len(pieces))], axis=1)
    put(0, jnp.where(state == 0, parents, kids[:ROWS]).astype(BF16))
    put(1, kids[ROWS:].astype(BF16))


def scratch_sets():
    wide = pltpu.VMEM((PART // LANES, PAD * FIELDS, LANES), F32)
    kids = pltpu.VMEM((PART // LANES, 2 * ROWS, LANES), F32)
    return [wide] * SETS + [kids] * SETS


def clear(wide_refs):
    for wide_ref in wide_refs:
        wide_ref[:, ROWS:, :] = jnp.zeros((PART // LANES, PAD * FIELDS - ROWS, LANES), F32)


def home_kernel(fixed_ref, state_ref, prolong_ref, out_ref, weights_ref, *scratch):
    wide_refs, kids_refs = scratch[:SETS], scratch[SETS:]
    t = pl.program_id(0)

    @pl.when(t == 0)
    def _():
        weights_ref[...] = joined_weights(prolong_ref)
        clear(wide_refs)

    for h in range(SETS):
        at = pl.ds(pl.multiple_of(t * (SETS * PART) + h * PART, PART), PART)

        def put(child, value, h=h):
            out_ref[child, :, h * PART : (h + 1) * PART] = value

        parents = fixed_ref[:ROWS, at].astype(F32)
        bisect_part(weights_ref[...], parents, state_ref[:, at], wide_refs[h], kids_refs[h], put)


def home_call(fixed, state, prolong, slots):
    count = fixed.shape[1]
    tile = SETS * PART
    return pl.pallas_call(
        home_kernel,
        grid=(count // tile,),
        in_specs=[VMEM_SPEC, VMEM_SPEC, VMEM_SPEC],
        out_specs=[
            pl.BlockSpec((2, ROWS, tile), lambda i: (0, 0, i)),
            pl.BlockSpec((2 * PAD, 6 * PAD), lambda i: (0, 0)),
        ],
        out_shape=[
            jax.ShapeDtypeStruct((2, ROWS, slots), BF16),
            jax.ShapeDtypeStruct((2 * PAD, 6 * PAD), BF16),
        ],
        scratch_shapes=scratch_sets(),
        compiler_params=pltpu.CompilerParams(vmem_limit_bytes=LIMIT),
        cost_estimate=pl.CostEstimate(
            flops=2 * 560 * 280 * count, bytes_accessed=6 * ROWS * count, transcendentals=0
        ),
        name="home",
    )(fixed, state, prolong)


def incoming_kernel(*refs):
    parts, weights_ref, out_hbm = refs[:6], refs[6], refs[8]
    wide_refs, kids_refs = refs[9 : 9 + SETS], refs[9 + SETS : 9 + 2 * SETS]
    out_ref, sems = refs[9 + 2 * SETS :]
    cap = parts[0].shape[1]
    first = out_hbm.shape[2] - 6 * cap
    clear(wide_refs)
    copies = []
    for k in range(6):
        block = parts[k][...].astype(F32)
        state = block[ROWS : ROWS + 1].astype(jnp.int32)

        def put(child, value, k=k):
            out_ref[k, child] = value

        h = k % SETS
        bisect_part(weights_ref[...], block[:ROWS], state, wide_refs[h], kids_refs[h], put)
        target = out_hbm.at[:, :, pl.ds(first + k * cap, cap)]
        copies.append(pltpu.make_async_copy(out_ref.at[k], target, sems.at[k]))
        copies[-1].start()
    for copy in copies:
        copy.wait()


def incoming_call(parts, weights, kept):
    return pl.pallas_call(
        incoming_kernel,
        in_specs=[VMEM_SPEC] * 7 + [HBM_SPEC],
        out_specs=HBM_SPEC,
        out_shape=jax.ShapeDtypeStruct(kept.shape, BF16),
        scratch_shapes=scratch_sets()
        + [pltpu.VMEM((6, 2, ROWS, PART), BF16), pltpu.SemaphoreType.DMA((6,))],
        input_output_aliases={7: 0},
        compiler_params=pltpu.CompilerParams(vmem_limit_bytes=LIMIT),
        name="incoming",
    )(*parts, weights, kept)


def shards(
    parents,
    refine,
    edge,
    move,
    face_owner,
    face_local,
    face_pair,
    face_orient,
    prolong,
    restrict,
    lift,
):
    count = parents.shape[2]
    slots = count + 6 * (count // 16)
    x = parents.reshape(ROWS, count)
    prolong = prolong.transpose(0, 2, 1, 3)
    owns = trace_call(x, face_owner, face_local, restrict.transpose(1, 0, 2))
    span2 = passed_along(owns[3], "gz", 1)
    span3 = passed_along(owns[2], "gz", -1)
    stream0 = passed_along(owns[1], "gx", 1)
    stream1 = passed_along(owns[0], "gx", -1)
    near = [stream0, stream1, span2, span3]
    own, meta, table, raised, place, code, state = plan_call(
        owns,
        face_owner,
        face_local,
        face_pair,
        face_orient,
        lift.transpose(2, 0, 1),
        move[None, :],
        refine[None, :],
        edge[None, :],
    )
    payload, *packs = correct_call(FORWARD, x, own, near, meta, table, raised, place, code)
    packs += pack_call(BACKWARD, payload, place)
    parts = [None] * 6
    for k, pack in zip(FORWARD + BACKWARD, packs):
        parts[k] = passed_along(pack, ("gx", "gz"), OFFSETS[k])
    kept, weights = home_call(payload, state, prolong, slots)
    out = incoming_call(parts, weights, kept)
    return out.reshape(2, MODES, FIELDS, slots)


def solution(mesh):
    whole = ("gx", "gz")
    side = P(None, whole, None)
    in_specs = (P(None, None, whole), P(whole), P(whole), P(whole), side, side, side, side, P(), P(), P())
    out_specs = P(None, None, None, whole)
    return jax.shard_map(shards, mesh=mesh, in_specs=in_specs, out_specs=out_specs, check_vma=False)
```

```python
import functools

import jax
import jax.numpy as jnp
from jax import lax
from jax.experimental import pallas as pl
from jax.experimental.pallas import tpu as pltpu
from jax.sharding import PartitionSpec as P

MODES = 35
FMODES = 15
FIELDS = 8
ROWS = MODES * FIELDS
NODE_ROWS = FMODES * FIELDS
PAD = 40
LANES = 128
BUCKET = 512
WINDOW = 256
PART = 256
SETS = 4
LIMIT = 30 << 20
OFFSETS = (1, 2, 3, -1, -2, -3)
FORWARD = (1, 2, 0)
BACKWARD = (4, 5, 3)
F32 = jnp.float32
BF16 = jnp.bfloat16
NT = (((1,), (1,)), ((), ()))


def passed_along(block, axis, distance):
    count = lax.axis_size(axis)
    return lax.ppermute(block, axis, [((i - distance) % count, i) for i in range(count)])


def face_table():
    nodes = [(a, b, 4 - a - b) for a in range(5) for b in range(5 - a)]
    index = {node: place for place, node in enumerate(nodes)}
    orders = [(0, 1, 2), (1, 2, 0), (2, 0, 1), (1, 0, 2), (0, 2, 1), (2, 1, 0)]
    return [[index[n[p[0]], n[p[1]], n[p[2]]] for n in nodes] for p in orders]


def iota(shape, dim):
    return lax.broadcasted_iota(jnp.int32, shape, dim)


def ones_where(mask):
    return jnp.where(mask, 1.0, 0.0).astype(BF16)


def match(rows, row):
    shape = (rows, row.shape[1])
    lines = lax.broadcasted_iota(jnp.int16, shape, 0)
    same = lines == jnp.broadcast_to(row.astype(jnp.int16), shape)
    return jnp.where(same, jnp.array(1, BF16), jnp.array(0, BF16))


def dot(a, b):
    return jnp.dot(a, b, preferred_element_type=F32)


def spread(small, rows, columns):
    height, width = small.shape
    left = ones_where(iota((rows, height), 0) // FIELDS == iota((rows, height), 1))
    right = ones_where(iota((width, columns), 0) == iota((width, columns), 1) // FIELDS)
    full = dot(dot(left, small).astype(BF16), right)
    same = iota((rows, columns), 0) % FIELDS == iota((rows, columns), 1) % FIELDS
    return jnp.where(same, full, 0.0)


VMEM_SPEC = pl.BlockSpec(memory_space=pltpu.VMEM)
SMEM_SPEC = pl.BlockSpec(memory_space=pltpu.SMEM)
HBM_SPEC = pl.BlockSpec(memory_space=pltpu.HBM)


def fetches(sources, targets, sems):
    copies = [pltpu.make_async_copy(a, b, sems.at[i]) for i, (a, b) in enumerate(zip(sources, targets))]
    for copy in copies:
        copy.start()
    return copies


def room(*arrays):
    buffers = [pltpu.VMEM(a.shape, a.dtype) for a in arrays]
    return buffers + [pltpu.SemaphoreType.DMA((len(arrays),))]


def trace_kernel(tile, *refs):
    sources, own_refs, every_ref, held, sems = refs[:4], refs[4:8], refs[8], refs[9:13], refs[13]
    restrict_ref, owner_ref, local_ref, x_ref = held
    copies = fetches(sources, held, sems)
    count = x_ref.shape[1]
    faces = owner_ref.shape[2]
    copies[0].wait()
    spreads = [spread(restrict_ref[:, l, :], NODE_ROWS, ROWS) for l in range(4)]
    every_ref[...] = jnp.concatenate(spreads, axis=0).astype(BF16)
    for copy in copies[1:]:
        copy.wait()
    for s in range(4):

        def step(j, carry, s=s):
            lanes = pl.ds(pl.multiple_of(j * tile, tile), tile)
            owner = owner_ref[s, :, lanes]
            local = local_ref[s, :, lanes]
            onehot = match(count, owner)
            picked = dot(x_ref[...], onehot).astype(BF16)
            traces = dot(every_ref[...], picked)
            chosen = traces[:NODE_ROWS]
            for l in range(1, 4):
                chosen = jnp.where(local == l, traces[l * NODE_ROWS : (l + 1) * NODE_ROWS], chosen)
            own_refs[s][:, lanes] = chosen.astype(BF16)
            return carry

        lax.fori_loop(0, faces // tile, step, 0)


def trace_call(x, owner, local, restrict):
    faces = owner.shape[2]
    return pl.pallas_call(
        functools.partial(trace_kernel, 1024),
        in_specs=[HBM_SPEC] * 4,
        out_specs=[VMEM_SPEC] * 4,
        out_shape=[jax.ShapeDtypeStruct((NODE_ROWS, faces), BF16)] * 4,
        scratch_shapes=[pltpu.VMEM((4 * NODE_ROWS, ROWS), BF16)] + room(restrict, owner, local, x),
        compiler_params=pltpu.CompilerParams(vmem_limit_bytes=LIMIT),
        cost_estimate=pl.CostEstimate(flops=10**10, bytes_accessed=10**7, transcendentals=0),
        name="trace",
    )(*[pltpu.with_memory_space_constraint(a, pltpu.HBM) for a in (restrict, owner, local, x)])


def rank_moves(move_ref, refine_ref, edge_ref, place_ref, code_ref, state_ref):
    count = move_ref.shape[1]
    block = 256
    cap = count // 16
    before = ones_where(iota((block, block), 0) < iota((block, block), 1))
    seen = jnp.zeros((8, 1), F32)
    which = iota((8, block), 0)
    for b in range(count // block):
        at = slice(b * block, (b + 1) * block)
        move = move_ref[:, at]
        hit = jnp.where(which == move, 1.0, 0.0)
        earlier = dot(hit.astype(BF16), before) + seen
        rank = jnp.sum(hit * earlier, axis=0, keepdims=True).astype(jnp.int32)
        place_ref[:, at] = jnp.where(move < 6, move * cap + rank, 6 * cap)
        seen = seen + jnp.sum(hit, axis=1, keepdims=True)
        code = jnp.where(refine_ref[:, at] == 1, edge_ref[:, at] + 1, 0)
        code_ref[:, at] = code
        state_ref[:, at] = jnp.where(move == 6, code, -1)


def plan_kernel(*refs):
    own_refs, sources, held, sems = refs[:4], refs[4:12], refs[19:27], refs[27]
    own_ref, meta_ref, table_ref, raised_ref, place_ref, code_ref, state_ref = refs[12:19]
    owner_ref, local_ref, pair_ref, orient_ref, lift_ref, move_ref, refine_ref, edge_ref = held
    for copy in fetches(sources, held, sems):
        copy.wait()
    rank_moves(move_ref, refine_ref, edge_ref, place_ref, code_ref, state_ref)
    raised = [spread(lift_ref[:, l, :].astype(BF16), NODE_ROWS, ROWS) for l in range(4)]
    raised_ref[...] = jnp.concatenate(raised, axis=0).T.astype(BF16)
    faces = owner_ref.shape[2]
    block = 256
    before = ones_where(iota((block, block), 0) < iota((block, block), 1))
    eight = iota((8, faces), 0)
    buckets = [owner_ref[s] // BUCKET for s in range(4)]
    hits = jnp.concatenate([jnp.where(eight == b, 1.0, 0.0) for b in buckets], axis=0)
    smaller = jnp.concatenate([jnp.where(b < eight, 1.0, 0.0) for b in buckets], axis=0)
    start = jnp.sum(smaller, axis=1, keepdims=True)
    end = start + jnp.sum(hits, axis=1, keepdims=True)
    first = start.astype(jnp.int32)
    last = end.astype(jnp.int32)
    begin = jnp.minimum(first // LANES * LANES, faces - LANES)
    trips = (last - begin + WINDOW - 1) // WINDOW
    longest = jnp.maximum(
        jnp.maximum(trips[0:8], trips[8:16]), jnp.maximum(trips[16:24], trips[24:32])
    )
    longest = jnp.concatenate([longest] * 4, axis=0)
    lane = iota((32, LANES), 1)
    table_ref[...] = jnp.where(lane == 0, begin, jnp.where(lane == 1, trips, longest))
    seen = start
    places = []
    for b in range(faces // block):
        part = hits[:, b * block : (b + 1) * block]
        places.append(part * (dot(part.astype(BF16), before) + seen))
        seen = seen + jnp.sum(part, axis=1, keepdims=True)
    places = jnp.concatenate(places, axis=1)
    meta_ref[...] = jnp.full(meta_ref.shape, -1, jnp.int32)
    for s in range(4):
        spot = jnp.sum(places[8 * s : 8 * s + 8], axis=0, keepdims=True).astype(jnp.int32)
        order = match(faces, spot)
        owner, pair = owner_ref[s], pair_ref[s]
        values = (owner // 256, owner % 256, local_ref[s], pair // 256, pair % 256, orient_ref[s])
        small = jnp.zeros((8, faces), jnp.int32)
        for row, value in enumerate(values):
            small = jnp.where(eight == row, value, small)
        both = jnp.concatenate([own_refs[s][...].astype(F32), small.astype(F32)], axis=0)
        moved = lax.dot_general(both.astype(BF16), order, NT, preferred_element_type=F32)
        own_ref[s] = moved[:NODE_ROWS].astype(BF16)
        got = moved[NODE_ROWS:].astype(jnp.int32)
        rows = (got[0:1] * 256 + got[1:2], got[2:3], got[3:4] * 256 + got[4:5], got[5:6])
        meta = jnp.zeros((8, faces), jnp.int32)
        for row, value in enumerate(rows):
            meta = jnp.where(eight == row, value, meta)
        meta_ref[s, :, :faces] = meta


def plan_call(owns, *rest):
    faces = rest[0].shape[2]
    flat = jax.ShapeDtypeStruct(rest[-1].shape, jnp.int32)
    return pl.pallas_call(
        plan_kernel,
        in_specs=[VMEM_SPEC] * 4 + [HBM_SPEC] * 8,
        out_specs=[VMEM_SPEC] * 7,
        out_shape=[
            jax.ShapeDtypeStruct((4, NODE_ROWS, faces), BF16),
            jax.ShapeDtypeStruct((4, 8, faces + LANES), jnp.int32),
            jax.ShapeDtypeStruct((32, LANES), jnp.int32),
            jax.ShapeDtypeStruct((ROWS, 4 * NODE_ROWS), BF16),
            flat,
            flat,
            flat,
        ],
        scratch_shapes=room(*rest),
        compiler_params=pltpu.CompilerParams(vmem_limit_bytes=LIMIT),
        cost_estimate=pl.CostEstimate(flops=5 * 10**9, bytes_accessed=4 * 10**6, transcendentals=0),
        name="plan",
    )(*owns, *rest)


def correct_kernel(tile, moves, *refs):
    raised_ref, x_hbm, own_ref = refs[:3]
    near_refs = refs[3:7]
    meta_ref, table_ref, place_ref, code_ref, payload_ref = refs[7:12]
    pack_refs = refs[12 : 12 + len(moves)]
    lifted_ref, total_ref, x_ref, sems = refs[12 + len(moves) :]
    copies = fetches((x_hbm,), (x_ref,), sems)
    count = x_ref.shape[1]
    faces = own_ref.shape[2]
    table = face_table()

    def jumps(j, carry):
        lanes = pl.ds(pl.multiple_of(j * tile, tile), tile)
        for s in range(4):
            local = meta_ref[s, 1:2, lanes]
            pair = meta_ref[s, 2:3, lanes]
            orient = meta_ref[s, 3:4, lanes]
            matcher = match(faces, pair)
            paired = dot(near_refs[s][...], matcher)
            own = own_ref[s, :, lanes].astype(F32)
            jump = []
            for n in range(FMODES):
                best = paired[table[0][n] * FIELDS : (table[0][n] + 1) * FIELDS]
                for o in range(1, 6):
                    if table[o][n] != table[0][n]:
                        other = paired[table[o][n] * FIELDS : (table[o][n] + 1) * FIELDS]
                        best = jnp.where(orient == o, other, best)
                jump.append(0.5 * (best - own[n * FIELDS : (n + 1) * FIELDS]))
            jump = jnp.concatenate(jump, axis=0)
            split = jnp.concatenate([jnp.where(local == l, jump, 0.0) for l in range(4)], axis=0)
            lifted_ref[s, :, lanes] = dot(raised_ref[...], split.astype(BF16)).astype(BF16)
        return carry

    for s in range(4):
        lifted_ref[s, :, faces:] = jnp.zeros((ROWS, LANES), BF16)
    lax.fori_loop(0, faces // tile, jumps, 0)
    copies[0].wait()

    def window(s, t, i):
        begin = table_ref[8 * s + t, 0] + i * WINDOW
        lanes = pl.ds(pl.multiple_of(begin, LANES), WINDOW)
        return lifted_ref[s, :, lanes], match(BUCKET, meta_ref[s, 0:1, lanes] - t * BUCKET)

    def fix(pair, carry):
        buckets = [2 * pair, 2 * pair + 1]
        spots = [pl.ds(pl.multiple_of(t * BUCKET, BUCKET), BUCKET) for t in buckets]
        for u, (t, at) in enumerate(zip(buckets, spots)):
            both = [window(s, t, 0) for s in range(4)]
            total_ref[u] = x_ref[:, at].astype(F32) + lax.dot_general(
                jnp.concatenate([a for a, _ in both], axis=1),
                jnp.concatenate([b for _, b in both], axis=1),
                NT,
                preferred_element_type=F32,
            )

        @pl.when(jnp.maximum(table_ref[buckets[0], 2], table_ref[buckets[1], 2]) > 1)
        def _():
            for u, t in enumerate(buckets):
                for s in range(4):

                    def more(i, carry, s=s, t=t, u=u):
                        a, b = window(s, t, i)
                        total_ref[u] += lax.dot_general(a, b, NT, preferred_element_type=F32)
                        return carry

                    lax.fori_loop(1, table_ref[8 * s + t, 1], more, 0)

        for u, at in enumerate(spots):
            code = jnp.broadcast_to(code_ref[:, at], (8, BUCKET)).astype(F32)
            payload_ref[:, at] = jnp.concatenate([total_ref[u], code], axis=0).astype(BF16)
        return carry

    lax.fori_loop(0, count // (2 * BUCKET), fix, 0)
    pack_moves(moves, payload_ref, place_ref, pack_refs)


def pack_moves(moves, payload_ref, place_ref, pack_refs):
    cap = pack_refs[0].shape[1]
    low = min(moves)
    packer = match(len(moves) * cap, place_ref[...] - low * cap)
    packed = lax.dot_general(payload_ref[...], packer, NT, preferred_element_type=F32)
    for k, pack_ref in zip(moves, pack_refs):
        pack_ref[...] = packed[:, (k - low) * cap : (k - low + 1) * cap].astype(BF16)


def pack_kernel(moves, payload_ref, place_ref, *pack_refs):
    pack_moves(moves, payload_ref, place_ref, pack_refs)


def pack_call(moves, payload, place):
    rows, count = payload.shape
    return pl.pallas_call(
        functools.partial(pack_kernel, moves),
        in_specs=[VMEM_SPEC] * 2,
        out_specs=[VMEM_SPEC] * len(moves),
        out_shape=[jax.ShapeDtypeStruct((rows, count // 16), BF16)] * len(moves),
        compiler_params=pltpu.CompilerParams(vmem_limit_bytes=LIMIT),
        cost_estimate=pl.CostEstimate(flops=2 * 10**9, bytes_accessed=10**6, transcendentals=0),
        name="pack",
    )(payload, place)


def correct_call(moves, x, own, near, meta, table, raised, place, code):
    count = x.shape[1]
    cap = count // 16
    faces = own.shape[2]
    rows = ROWS + 8
    return pl.pallas_call(
        functools.partial(correct_kernel, 1024, moves),
        in_specs=[VMEM_SPEC, HBM_SPEC] + [VMEM_SPEC] * 6 + [SMEM_SPEC] + [VMEM_SPEC] * 2,
        out_specs=[VMEM_SPEC] * (1 + len(moves)),
        out_shape=[jax.ShapeDtypeStruct((rows, count), BF16)]
        + [jax.ShapeDtypeStruct((rows, cap), BF16)] * len(moves),
        scratch_shapes=[
            pltpu.VMEM((4, ROWS, faces + LANES), BF16),
            pltpu.VMEM((2, ROWS, BUCKET), F32),
        ]
        + room(x),
        compiler_params=pltpu.CompilerParams(vmem_limit_bytes=LIMIT),
        cost_estimate=pl.CostEstimate(flops=10**10, bytes_accessed=10**7, transcendentals=0),
        name="correct",
    )(raised, x, own, *near, meta, table, place, code)


def joined_weights(prolong_ref):
    rows = []
    for c in range(2):
        total = jnp.zeros((PAD, 6 * PAD), F32)
        for e in range(6):
            left = ones_where(iota((PAD, MODES), 0) == iota((PAD, MODES), 1))
            right = ones_where(iota((MODES, 6 * PAD), 0) + e * PAD == iota((MODES, 6 * PAD), 1))
            total += dot(dot(left, prolong_ref[e, :, c, :]).astype(BF16), right)
        rows.append(total)
    return jnp.concatenate(rows, axis=0).astype(BF16)


def bisect_part(weights, parents, state, wide_ref, kids_ref, put):
    pieces = [slice(i * LANES, (i + 1) * LANES) for i in range(PART // LANES)]
    parents = jnp.where(state >= 0, parents, 0.0)
    shape = (2 * PAD, PART)
    second = (iota(shape, 0) // PAD).astype(jnp.int16)
    cut = jnp.broadcast_to((state - 1).astype(jnp.int16), shape) - second
    for i, piece in enumerate(pieces):
        wide_ref[i, :ROWS, :] = parents[:, piece]
    for f in range(FIELDS):
        modes = [wide_ref[i, pl.ds(f, PAD, stride=FIELDS), :] for i in range(len(pieces))]
        modes = jnp.concatenate(modes, axis=1)
        twice = jnp.concatenate([modes, modes], axis=0).astype(BF16)
        masked = [jnp.where(cut == 2 * i, twice, jnp.array(0, BF16)) for i in range(3)]
        both = dot(weights, jnp.concatenate(masked, axis=0))
        for i, piece in enumerate(pieces):
            kids_ref[i, pl.ds(f, MODES, stride=FIELDS), :] = both[:MODES, piece]
            kids_ref[i, pl.ds(ROWS + f, MODES, stride=FIELDS), :] = both[PAD : PAD + MODES, piece]
    kids = jnp.concatenate([kids_ref[i] for i in range(len(pieces))], axis=1)
    put(0, jnp.where(state == 0, parents, kids[:ROWS]).astype(BF16))
    put(1, kids[ROWS:].astype(BF16))


def scratch_sets():
    wide = pltpu.VMEM((PART // LANES, PAD * FIELDS, LANES), F32)
    kids = pltpu.VMEM((PART // LANES, 2 * ROWS, LANES), F32)
    return [wide] * SETS + [kids] * SETS


def clear(wide_refs):
    for wide_ref in wide_refs:
        wide_ref[:, ROWS:, :] = jnp.zeros((PART // LANES, PAD * FIELDS - ROWS, LANES), F32)


def home_kernel(fixed_ref, state_ref, prolong_ref, out_ref, weights_ref, *scratch):
    wide_refs, kids_refs = scratch[:SETS], scratch[SETS:]
    t = pl.program_id(0)

    @pl.when(t == 0)
    def _():
        weights_ref[...] = joined_weights(prolong_ref)
        clear(wide_refs)

    for h in range(SETS):
        at = pl.ds(pl.multiple_of(t * (SETS * PART) + h * PART, PART), PART)

        def put(child, value, h=h):
            out_ref[child, :, h * PART : (h + 1) * PART] = value

        parents = fixed_ref[:ROWS, at].astype(F32)
        bisect_part(weights_ref[...], parents, state_ref[:, at], wide_refs[h], kids_refs[h], put)


def home_call(fixed, state, prolong, slots):
    count = fixed.shape[1]
    tile = SETS * PART
    return pl.pallas_call(
        home_kernel,
        grid=(count // tile,),
        in_specs=[VMEM_SPEC, VMEM_SPEC, VMEM_SPEC],
        out_specs=[
            pl.BlockSpec((2, ROWS, tile), lambda i: (0, 0, i)),
            pl.BlockSpec((2 * PAD, 6 * PAD), lambda i: (0, 0)),
        ],
        out_shape=[
            jax.ShapeDtypeStruct((2, ROWS, slots), BF16),
            jax.ShapeDtypeStruct((2 * PAD, 6 * PAD), BF16),
        ],
        scratch_shapes=scratch_sets(),
        compiler_params=pltpu.CompilerParams(vmem_limit_bytes=LIMIT),
        cost_estimate=pl.CostEstimate(
            flops=2 * 560 * 280 * count, bytes_accessed=6 * ROWS * count, transcendentals=0
        ),
        name="home",
    )(fixed, state, prolong)


def incoming_kernel(*refs):
    parts, weights_ref, out_hbm = refs[:6], refs[6], refs[8]
    wide_refs, kids_refs = refs[9 : 9 + SETS], refs[9 + SETS : 9 + 2 * SETS]
    out_ref, sems = refs[9 + 2 * SETS :]
    cap = parts[0].shape[1]
    first = out_hbm.shape[2] - 6 * cap
    clear(wide_refs)
    copies = []
    for k in range(6):
        block = parts[k][...].astype(F32)
        state = block[ROWS : ROWS + 1].astype(jnp.int32)

        def put(child, value, k=k):
            out_ref[k, child] = value

        h = k % SETS
        bisect_part(weights_ref[...], block[:ROWS], state, wide_refs[h], kids_refs[h], put)
        target = out_hbm.at[:, :, pl.ds(first + k * cap, cap)]
        copies.append(pltpu.make_async_copy(out_ref.at[k], target, sems.at[k]))
        copies[-1].start()
    for copy in copies:
        copy.wait()


def incoming_call(parts, weights, kept):
    return pl.pallas_call(
        incoming_kernel,
        in_specs=[VMEM_SPEC] * 7 + [HBM_SPEC],
        out_specs=HBM_SPEC,
        out_shape=jax.ShapeDtypeStruct(kept.shape, BF16),
        scratch_shapes=scratch_sets()
        + [pltpu.VMEM((6, 2, ROWS, PART), BF16), pltpu.SemaphoreType.DMA((6,))],
        input_output_aliases={7: 0},
        compiler_params=pltpu.CompilerParams(vmem_limit_bytes=LIMIT),
        name="incoming",
    )(*parts, weights, kept)


def shards(
    parents,
    refine,
    edge,
    move,
    face_owner,
    face_local,
    face_pair,
    face_orient,
    prolong,
    restrict,
    lift,
):
    count = parents.shape[2]
    slots = count + 6 * (count // 16)
    x = parents.reshape(ROWS, count)
    prolong = prolong.transpose(0, 2, 1, 3)
    owns = trace_call(x, face_owner, face_local, restrict.transpose(1, 0, 2))
    span2 = passed_along(owns[3], "gz", 1)
    span3 = passed_along(owns[2], "gz", -1)
    stream0 = passed_along(owns[1], "gx", 1)
    stream1 = passed_along(owns[0], "gx", -1)
    near = [stream0, stream1, span2, span3]
    own, meta, table, raised, place, code, state = plan_call(
        owns,
        face_owner,
        face_local,
        face_pair,
        face_orient,
        lift.transpose(2, 0, 1),
        move[None, :],
        refine[None, :],
        edge[None, :],
    )
    payload, *packs = correct_call(FORWARD, x, own, near, meta, table, raised, place, code)
    packs += pack_call(BACKWARD, payload, place)
    parts = [None] * 6
    for k, pack in zip(FORWARD + BACKWARD, packs):
        parts[k] = passed_along(pack, ("gx", "gz"), OFFSETS[k])
    kept, weights = home_call(payload, state, prolong, slots)
    out = incoming_call(parts, weights, kept)
    return out.reshape(2, MODES, FIELDS, slots)


def solution(mesh):
    whole = ("gx", "gz")
    side = P(None, whole, None)
    in_specs = (P(None, None, whole), P(whole), P(whole), P(whole), side, side, side, side, P(), P(), P())
    out_specs = P(None, None, None, whole)
    return jax.shard_map(shards, mesh=mesh, in_specs=in_specs, out_specs=out_specs, check_vma=False)
```
